256 devices in a mesh: grp: 2 (over z), tp: 128 (over y, x, core).
Axes of the slice: x: 8, y: 8, z: 2, core: 2. Of those that a mesh axis runs over, the one named last changes fastest.
The devices are a block of a 8x8x16 slice.
Arguments:
- hidden: bfloat16 [1024, 16384], P('grp', 'tp'), parts along dimension 0, may hold values from -36 to 36
- norm_gain: float32 [16384], P('tp'), may hold values from 0.3 to 10, as said below
- prefix: int32 [2], P('grp'), parts along dimension 0, may hold values from 0 to 8192
- w_query: bfloat16 [16384, 16384], P(None, 'tp'), may hold values from -0.046875 to 0.046875
- w_kv: bfloat16 [2048, 16384], P('tp'), may hold values from -0.046875 to 0.046875
- w_scale: float32 [18432], P('tp'), may hold values from 0.25 to 4
Outputs:
- queries: bfloat16 [1024, 16384], P('grp', 'tp'), parts along dimension 0
- keys: bfloat16 [1024, 16384], P('grp', 'tp'), parts along dimension 0
- values: bfloat16 [1024, 16384], P('grp', 'tp'), parts along dimension 0
- payload: bfloat16 [1024, 16384], P('grp', 'tp'), parts along dimension 0
- row_scale: float32 [1024], P('grp'), parts along dimension 0
The draws below stay inside these ranges and needn't reach their ends.
There are 2 independent parts, one for each index of `grp`. The reference program is written for one: setup_inputs(seed, part) draws one part's arguments, and reference() takes and returns one part's arrays. A program takes and returns all parts, laid end to end along the dimension named above; an argument that names none is the same for every part. Nothing has to cross between parts.
Inputs may be any that keep to these rules, and one draw needn't show every extreme that they name: `norm_gain`: positive.
All inputs are finite; a program needn't handle non-finite values. Where the reference program divides by a largest or mean magnitude, that divisor is 1e-20 or more.
Results may differ from the reference program's by a relative error of at most 0.012.
Values may be sent and summed in bfloat16 or wider, within the bound.
A program may use at most 64 MiB of HBM per device.

```python
import math
import jax
import jax.numpy as jnp
from jax import lax

D = 16384
HD = 128
HQ_DEV = 1
KV_COLS_DEV = 8
TOKENS = 512
PREFIX_MAX = 8192
H = 128
KVH = 8
COLS_DEV = 144
N_TP = 128


def draw_norm_gain(key, part):
    columns = jnp.arange(D, dtype=jnp.float32)
    rising = 1.0 + 2.0 * columns / (D - 1)
    rough = jnp.exp(jax.random.uniform(key, (D,), jnp.float32, -0.7, 0.7))
    return rising * rough


def draw_hidden(key, part):
    columns = jnp.arange(D, dtype=jnp.float32) / (D - 1)
    noise = jax.random.normal(jax.random.fold_in(key, 11), (TOKENS, D), jnp.float32)
    noise = jnp.clip(noise, -6.0, 6.0)
    column_scale = 0.5 + columns
    values = noise * column_scale[None, :]
    return values.astype(jnp.bfloat16)


def steps_of(stream_key, shape, split, smallest, top_value):
    factor_of, own = 1.0, jax.random.fold_in(stream_key, 6)
    for position, blocks in split:
        steps = jnp.exp(jax.random.uniform(jax.random.fold_in(own, position), (blocks,), jnp.float32, smallest / len(split), top_value / len(split)))
        factor_of = factor_of * jnp.repeat(steps, shape[position] // blocks).reshape([-1 if axis == position else 1 for axis in range(len(shape))])
    return factor_of


def bell_draw(own_key, dims, scale, bound, shards=(), kind=jnp.bfloat16):
    level = steps_of(own_key, dims, shards, -0.22, 0.18) if shards else 1.0
    array = jax.random.normal(own_key, dims, jnp.float32) * scale * level
    return jnp.minimum(jnp.maximum(array, -bound), bound).astype(kind)


def setup_inputs(seed: int = 0, part: int = 0) -> dict:
    splits = jax.random.split(jax.random.key(seed), 7)
    part_keys = jax.random.split(jax.random.fold_in(splits[6], part), 7)
    return {
        "hidden": draw_hidden(jax.random.fold_in(jax.random.fold_in(splits[6], part), 71), part),
        "norm_gain": draw_norm_gain(jax.random.fold_in(splits[6], 71), part),
        "prefix": jax.random.randint(part_keys[2], (1,), 0, PREFIX_MAX + 1).astype(jnp.int32),
        "w_query": bell_draw(splits[3], (D, H * HD), D ** -0.5, 0.046875, ((1, 128),)),
        "w_kv": bell_draw(splits[4], (N_TP * 2 * KV_COLS_DEV, D), D ** -0.5, 0.046875, ((0, 128),)),
        "w_scale": jnp.clip(jnp.exp(math.log(4.0) - 2.7725887 * jax.random.uniform(splits[5], (N_TP * COLS_DEV,), jnp.float32) ** steps_of(splits[5], (N_TP * COLS_DEV,), ((0, 128),), -0.2, 0.2)), 0.25, 4.0),
    }


norm_eps = 1e-05
tiny_eps = 1e-06
rope_base = 500000.0

def rotate(matrix, positions, offset):
    count, width = matrix.shape
    pairs = matrix.reshape(count, width // 2, 2)
    columns = offset + 2 * jnp.arange(width // 2, dtype=jnp.int32)
    pair_index = (columns % HD // 2).astype(jnp.float32)
    inverse_freq = jnp.power(jnp.float32(rope_base), -(2.0 * pair_index) / HD)
    angle = positions.astype(jnp.float32)[:, None] * inverse_freq[None, :]
    cosine = jnp.cos(angle)
    sine = jnp.sin(angle)
    first = pairs[:, :, 0]
    second = pairs[:, :, 1]
    turned = jnp.stack([first * cosine - second * sine, second * cosine + first * sine], axis=-1)
    return turned.reshape(count, width)

def repeat_heads(matrix):
    heads = matrix.reshape(TOKENS, KVH, 1, HD)
    spread = jnp.broadcast_to(heads, (TOKENS, KVH, N_TP // KVH, HD)).reshape(TOKENS, N_TP, 1, HD)
    spread = jnp.broadcast_to(spread, (TOKENS, N_TP, HQ_DEV, HD))
    return spread.reshape(TOKENS, N_TP * HQ_DEV * HD)

def head_order(blocks):
    pieces = N_TP // KVH
    grouped = blocks.reshape(TOKENS, pieces, KVH, KV_COLS_DEV)
    return jnp.transpose(grouped, (0, 2, 1, 3)).reshape(TOKENS, KVH * HD)

def reference(hidden, norm_gain, prefix, w_query, w_kv, w_scale):
    widened = hidden.astype(jnp.float32)
    square_sum = lax.optimization_barrier(jnp.sum(widened * widened, axis=1))
    inverse = 1.0 / jnp.sqrt(square_sum / D + norm_eps)
    weighted = widened * norm_gain[None, :]
    normed = weighted * inverse[:, None]
    row_scale = lax.optimization_barrier(jnp.max(jnp.abs(normed), axis=1)) + tiny_eps
    payload = (normed / row_scale[:, None]).astype(jnp.bfloat16)
    qwidth = HQ_DEV * HD
    query_raw = jnp.dot(payload, w_query, preferred_element_type=jnp.float32)
    kv_raw = jnp.dot(payload, w_kv.T, preferred_element_type=jnp.float32)
    raw = jnp.concatenate([query_raw.reshape(TOKENS, N_TP, qwidth), kv_raw.reshape(TOKENS, N_TP, 2 * KV_COLS_DEV)], axis=2)
    blocks = raw * row_scale[:, None, None] * w_scale.reshape(1, N_TP, COLS_DEV)
    query_cols = blocks[:, :, :qwidth].reshape(TOKENS, N_TP * qwidth)
    key_cols = head_order(blocks[:, :, qwidth:qwidth + KV_COLS_DEV])
    value_cols = head_order(blocks[:, :, qwidth + KV_COLS_DEV:])
    positions = prefix[0] + jnp.arange(TOKENS, dtype=jnp.int32)
    queries = rotate(query_cols, positions, 0).astype(jnp.bfloat16)
    rotated_keys = rotate(key_cols, positions, 0).astype(jnp.bfloat16)
    value_round = value_cols.astype(jnp.bfloat16)
    keys = repeat_heads(rotated_keys)
    values = repeat_heads(value_round)
    return (queries, keys, values, payload, row_scale)
```

```python
import functools
import heapq
import math

import jax
import jax.numpy as jnp
from jax import lax
from jax.experimental import pallas as pl
from jax.experimental.pallas import tpu as pltpu
from jax.sharding import PartitionSpec as P

HD = 128
KVC = 8
norm_eps = 1e-05
tiny_eps = 1e-06
rope_base = 500000.0

ROUNDS = 1
GROUP = 4
LEAD = 3.0
W_READY = 14.0
STEP = {"R": (0, 1), "L": (0, -1), "U": (1, 0), "D": (-1, 0)}
LINKS = "RLUD"


def plan(side, rounds, unit, lat=1.5):
    half = side // 2

    def signed(v):
        v %= side
        return v - side if v >= half else v

    def onward(kind, dy, dx, via):
        if kind in "SC":
            a, b = (dx, 0) if kind == "S" else (dy, 0)
        else:
            a, b = (dx, dy) if kind == "A" else (dy, dx)
        f1, b1, f2, b2 = ("R", "L", "U", "D") if kind in "AS" else ("U", "D", "R", "L")
        second = [f2, b2] if kind in "AB" else []
        if via is None:
            return [f1, b1] + second
        if b == 0:
            if via == f1 and a > -half:
                return [f1] + second
            if via == b1 and 0 < a < half - 1:
                return [b1] + second
            return second
        if b == -half:
            return []
        if via == f2 and (-b < half - 1 or a < 0):
            return [f2]
        if via == b2 and (b < half - 1 or (b == half - 1 and a >= 0)):
            return [b2]
        return []

    pending = {link: [] for link in LINKS}
    free = {link: 0.0 for link in LINKS}
    count = {link: 0 for link in LINKS}
    actions, heap, tick = [], [], [0]

    def push(time, what):
        tick[0] += 1
        heapq.heappush(heap, (time, tick[0], what))

    def offer(chunk, via, now):
        for link in onward(chunk[0], chunk[2], chunk[3], via):
            tick[0] += 1
            rank = -1 if chunk[0] in "SC" else chunk[1]
            heapq.heappush(pending[link], (rank, tick[0], now, chunk))
            push(now, ("link", link))

    for rnd in range(rounds):
        for kind in "AB":
            offer((kind, rnd, 0, 0), None, 0.0)
    push(0.6, ("stat", "S"))
    left = {"S": side - 1, "C": side - 1}
    arrived = {}
    seen = set()
    while heap:
        now, _, what = heapq.heappop(heap)
        if what[0] == "link":
            link = what[1]
            if not pending[link]:
                continue
            if free[link] > now + 1e-9:
                push(free[link], what)
                continue
            _, _, ready, chunk = heapq.heappop(pending[link])
            took = 0.1 if chunk[0] in "SC" else unit
            free[link] = now + took
            k = count[link]
            count[link] += 1
            actions.append((max(ready, now - LEAD), ("send", link, k, chunk)))
            oy, ox = STEP[link]
            there = (chunk[0], chunk[1], signed(chunk[2] - oy), signed(chunk[3] - ox))
            push(free[link] + lat, ("arrive", link, k, there))
            if pending[link]:
                push(free[link], what)
        elif what[0] == "arrive":
            _, link, k, chunk = what
            assert chunk not in seen
            seen.add(chunk)
            actions.append((now, what))
            offer(chunk, link, now)
            if chunk[0] in "SC":
                left[chunk[0]] -= 1
                if left[chunk[0]] == 0:
                    actions.append((now, ("total", chunk[0])))
                    if chunk[0] == "S":
                        push(now + 0.3, ("stat", "C"))
            else:
                arrived.setdefault((chunk[1], chunk[0]), []).append((now, chunk))
        elif what[0] == "stat":
            offer((what[1], 0, 0, 0), None, now)
    assert len(seen) == 2 * rounds * (side * side - 1) + 2 * (side - 1)
    tasks = []
    for (rnd, kind), got in arrived.items():
        got = [(0.0, (kind, rnd, 0, 0))] + got
        for at in range(0, len(got), GROUP):
            part = got[at : at + GROUP]
            tasks.append((part[-1][0], rnd, ("product", kind, rnd, at == 0, [c[2:] for _, c in part])))
    tasks.sort(key=lambda t: (t[0], t[1]))
    clock = W_READY
    for ready, _, task in tasks:
        clock = max(clock + 0.45, ready)
        actions.append((clock, task))
    last = {}
    for time, what in actions:
        if what[0] == "product":
            last[what[2]] = max(last.get(what[2], 0.0), time)
    end = max(t for t, _ in actions)
    for rnd, time in last.items():
        actions.append((time, ("partial", rnd)))
        actions.append((time + 1.8 if time < end - 3 else end + 1, ("share", rnd)))
    order = sorted(range(len(actions)), key=lambda i: (actions[i][0], i))
    return [actions[i][1] for i in order], count


def swap_pairs(x, axis):
    size = x.shape[axis]
    even = lax.broadcasted_iota(jnp.int32, x.shape, axis) % 2 == 0
    return jnp.where(even, pltpu.roll(x, size - 1, axis), pltpu.roll(x, 1, axis))


def frequency(columns):
    index = ((columns % HD) // 2).astype(jnp.float32)
    return jnp.exp2(index * (-2.0 * math.log2(rope_base) / HD))


def body(
    side, rounds, acts, count, width, kv_heads,
    prefix, h_ref, g_ref, ws_ref, wq_ref, wkv_ref,
    q_out, k_out, v_out, p_out, rs_out,
    xs, w_own, w_oth, kv_own, kv_oth, acc_q, acc_kv, part_q, part_kv,
    stat_row, stat_col, stat_oth, stat_t, cos_q, sin_q, share, heads,
    send_sem, recv_sem, local_sem, pair_send, pair_recv, share_send, share_recv,
):
    tokens = h_ref.shape[0]
    blocks = tokens // 128
    span = tokens // rounds
    half = span // 2
    me = lax.axis_index("tp")
    core = me % 2
    x = (me // 2) % side
    y = me // (2 * side)
    MESH = pl.DeviceIdType.MESH

    def device(yy, xx, cc):
        return {"tp": (yy * side + xx) * 2 + cc}

    partner = device(y, x, 1 - core)

    def slot_of(dy, dx):
        return ((y + dy + side) % side) * side + (x + dx + side) % side

    near = {
        link: device((y + oy + side) % side, (x + ox + side) % side, core)
        for link, (oy, ox) in STEP.items()
    }
    barrier = pltpu.get_barrier_semaphore()
    for target in list(near.values()) + [partner]:
        pl.semaphore_signal(barrier, inc=1, device_id=target, device_id_type=MESH)

    own_w = pltpu.make_async_copy(wq_ref.at[:, core], w_own, local_sem.at[0])
    own_kv = pltpu.make_async_copy(wkv_ref, kv_own, local_sem.at[1])
    own_w.start()
    own_kv.start()

    gain = g_ref[...]
    mine = slot_of(0, 0)
    for b in range(blocks):
        rows = slice(b * 128, (b + 1) * 128)
        xs[mine, rows, :] = (h_ref[rows, :].astype(jnp.float32) * gain).astype(jnp.bfloat16)

    pl.semaphore_wait(barrier, 5)

    def remote(src, dst, ssem, rsem, target):
        return pltpu.make_async_remote_copy(
            src_ref=src, dst_ref=dst, send_sem=ssem, recv_sem=rsem, device_id=target, device_id_type=MESH
        )

    give_kv = remote(wkv_ref, kv_oth, pair_send.at[0], pair_recv.at[0], partner)
    give_w = remote(wq_ref.at[:, 1 - core], w_oth, pair_send.at[1], pair_recv.at[1], partner)

    def tokens_of(kind, rnd):
        return rnd * span + (half if kind == "B" else 0)

    def place(chunk):
        kind, rnd, dy, dx = chunk
        if kind == "S":
            return stat_row.at[(x + dx + side) % side]
        if kind == "C":
            return stat_col.at[(y + dy + side) % side]
        return xs.at[slot_of(dy, dx), pl.ds(tokens_of(kind, rnd), half), :]

    def hop(link, k, chunk):
        ref = place(chunk)
        return remote(ref, ref, send_sem.at[LINKS.index(link), k], recv_sem.at[LINKS.index(link), k], near[link])

    def statistics():
        lane = lax.broadcasted_iota(jnp.int32, (128, 128), 1)
        total = jnp.zeros((128, 128), jnp.float32)
        for b in range(blocks):
            rows = slice(b * 128, (b + 1) * 128)
            wide = h_ref[rows, :].astype(jnp.float32)
            squares = jnp.sum(wide * wide, axis=1, keepdims=True)
            peak = jnp.max(jnp.abs(wide * gain), axis=1, keepdims=True)
            total = jnp.where(lane == 2 * b, squares, total)
            total = jnp.where(lane == 2 * b + 1, peak, total)
        stat_row[x] = jnp.transpose(total)[:8]

    def joined(a, b):
        even = lax.broadcasted_iota(jnp.int32, (8, 128), 0) % 2 == 0
        return jnp.where(even, a + b, jnp.maximum(a, b))

    def angles(b):
        rows = slice(b * 128, (b + 1) * 128)
        pos = prefix[0] + b * 128 + lax.broadcasted_iota(jnp.int32, (128, 128), 0)
        col = lax.broadcasted_iota(jnp.int32, (128, 128), 1)
        angle = pos.astype(jnp.float32) * frequency(col)
        sine = jnp.sin(angle)
        cos_q[rows, :] = jnp.cos(angle)
        sin_q[rows, :] = jnp.where(col % 2 == 0, -sine, sine)

    def product(kind, rnd, first, places):
        t0 = tokens_of(kind, rnd)
        slots = [slot_of(*p) for p in places]
        left = jnp.concatenate([xs[s, t0 : t0 + half, :] for s in slots], axis=1)
        right = jnp.concatenate([jnp.concatenate([w_own[s], w_oth[s]], axis=1) for s in slots], axis=0)
        out = jnp.dot(left, right, preferred_element_type=jnp.float32)
        starts = [pl.multiple_of((s * 2 + core) * width, width) for s in slots]
        rows_kv = jnp.concatenate(
            [jnp.concatenate([r[:, pl.ds(c, width)] for c in starts], axis=1) for r in (kv_own, kv_oth)], axis=0
        )
        kv = lax.dot_general(rows_kv, left, (((1,), (1,)), ((), ())), preferred_element_type=jnp.float32)
        for who in range(2):
            piece = out[:, who * HD : (who + 1) * HD]
            kvp = kv[who * 2 * KVC : (who + 1) * 2 * KVC]
            if first:
                acc_q[who, t0 : t0 + half, :] = piece
                acc_kv[who, :, t0 : t0 + half] = kvp
            else:
                acc_q[who, t0 : t0 + half, :] += piece
                acc_kv[who, :, t0 : t0 + half] += kvp

    def pair_copy(rnd, what):
        rng = pl.ds(rnd * span, span)
        if what == "kv":
            return remote(
                acc_kv.at[1, :, rng], part_kv.at[:, rng], pair_send.at[2 + rnd], pair_recv.at[2 + rnd], partner
            )
        at = 2 + rounds + rnd
        return remote(acc_q.at[1, rng, :], part_q.at[rng, :], pair_send.at[at], pair_recv.at[at], partner)

    give_stat = remote(
        stat_t, stat_oth, pair_send.at[2 + 2 * rounds], pair_recv.at[2 + 2 * rounds], partner
    )

    piece_me = me // kv_heads
    members = 2 * side * side // kv_heads
    head_to = me % kv_heads
    head_me = me // members

    def share_copy(rnd, m):
        rng = pl.ds(rnd * span, span)
        target = head_to * members + (m + me) % members
        return target, remote(
            share.at[:, rng], heads.at[piece_me, :, rng], share_send.at[rnd, m], share_recv.at[rnd, piece_me],
            {"tp": target},
        )

    ws_row = ws_ref[:, :HD]

    def share_round(rnd):
        rng = slice(rnd * span, (rnd + 1) * span)
        pair_copy(rnd, "kv").wait_recv()
        eye = lax.broadcasted_iota(jnp.int32, (2 * KVC, 2 * KVC), 0) == lax.broadcasted_iota(
            jnp.int32, (2 * KVC, 2 * KVC), 1
        )
        ws_col = jnp.sum(jnp.where(eye, ws_ref[:, HD:], 0.0), axis=1, keepdims=True)
        kv = (acc_kv[0, :, rng] + part_kv[:, rng]) * ws_col
        key, value = kv[:KVC], kv[KVC:]
        pos = prefix[0] + rnd * span + lax.broadcasted_iota(jnp.int32, (KVC, span), 1)
        row = lax.broadcasted_iota(jnp.int32, (KVC, span), 0)
        angle = pos.astype(jnp.float32) * frequency(piece_me * KVC + row)
        sine = jnp.sin(angle)
        key = key * jnp.cos(angle) + swap_pairs(key, 0) * jnp.where(row % 2 == 0, -sine, sine)
        both = jnp.concatenate([key, value], axis=0).astype(jnp.bfloat16)
        share[:, rng] = both

        @pl.when(head_to == head_me)
        def _():
            heads[piece_me, :, rng] = both

        for m in range(members):
            target, copy = share_copy(rnd, m)

            @pl.when(target != me)
            def _():
                copy.start()

    give_kv.start()
    give_w.start()
    started = weighed = False
    for act in acts:
        if act[0] == "send":
            _, link, k, chunk = act
            if chunk[0] == "S" and not started:
                started = True
                statistics()
            hop(link, k, chunk).start()
        elif act[0] == "arrive":
            _, link, k, chunk = act
            hop(link, k, chunk).wait_recv()
        elif act[0] == "total":
            if act[1] == "S":
                total = stat_row[0]
                for i in range(1, side):
                    total = joined(total, stat_row[i])
                stat_col[y] = total
                for b in range(blocks):
                    angles(b)
            else:
                total = stat_col[0]
                for i in range(1, side):
                    total = joined(total, stat_col[i])
                stat_t[...] = total
                give_stat.start()
        elif act[0] == "product":
            if not weighed:
                weighed = True
                own_w.wait()
                own_kv.wait()
                give_kv.wait_recv()
                give_w.wait_recv()
            product(*act[1:])
        elif act[0] == "partial":
            pair_copy(act[1], "kv").start()
            pair_copy(act[1], "q").start()
        elif act[0] == "share":
            share_round(act[1])

    give_stat.wait_recv()
    total = joined(stat_t[...], stat_oth[...])
    inverse = 1.0 / jnp.sqrt(total / (width * 2 * side * side) + norm_eps)
    even = lax.broadcasted_iota(jnp.int32, (8, 128), 0) % 2 == 0
    both = jnp.where(even, inverse, total * pltpu.roll(inverse, 1, 0) + tiny_eps)
    rs_out[...] = jnp.concatenate([both[2 * b + 1 : 2 * b + 2] for b in range(blocks)], axis=0)
    columns = jnp.transpose(jnp.concatenate([both, jnp.zeros((120, 128), jnp.float32)], axis=0))
    inv = [columns[:, 2 * b : 2 * b + 1] for b in range(blocks)]
    for b in range(blocks):
        rows = slice(b * 128, (b + 1) * 128)
        weighted = h_ref[rows, :].astype(jnp.float32) * gain
        p_out[rows, :] = ((weighted * inv[b]) / columns[:, 2 * b + 1 : 2 * b + 2]).astype(jnp.bfloat16)

    for rnd in range(rounds):
        pair_copy(rnd, "q").wait_recv()
    for b in range(blocks):
        rows = slice(b * 128, (b + 1) * 128)
        q = (acc_q[0, rows, :] + part_q[rows, :]) * ws_row * inv[b]
        q_out[rows, :] = (q * cos_q[rows, :] + swap_pairs(q, 1) * sin_q[rows, :]).astype(jnp.bfloat16)

    for rnd in range(rounds):
        for p in range(members):
            source = p * kv_heads + head_me
            rng = pl.ds(rnd * span, span)

            @pl.when(source != me)
            def _():
                remote(
                    heads.at[p, :, rng], heads.at[p, :, rng], share_send.at[rnd, 0], share_recv.at[rnd, p], partner
                ).wait_recv()

    for b in range(blocks):
        rows = slice(b * 128, (b + 1) * 128)
        got = [heads[p, :, rows].astype(jnp.float32) for p in range(members)]
        for out, at in ((k_out, 0), (v_out, KVC)):
            turned = jnp.transpose(jnp.concatenate([g[at : at + KVC] for g in got], axis=0))
            out[rows, :] = (turned * inv[b]).astype(jnp.bfloat16)

    for act in acts:
        if act[0] == "send":
            hop(*act[1:]).wait_send()
    give_kv.wait_send()
    give_w.wait_send()
    give_stat.wait_send()
    for rnd in range(rounds):
        pair_copy(rnd, "kv").wait_send()
        pair_copy(rnd, "q").wait_send()
        for m in range(members):
            target, copy = share_copy(rnd, m)

            @pl.when(target != me)
            def _():
                copy.wait_send()


def local(tp, hidden, norm_gain, prefix, w_query, w_kv, w_scale):
    tokens, width = hidden.shape
    side = math.isqrt(tp // 2)
    kv_heads = KVC * tp // HD
    members = tp // kv_heads
    rounds = ROUNDS
    acts, count = plan(side, rounds, 1.41 / rounds)
    most = max(count.values())
    chips = tp // 2
    bf, f32 = jnp.bfloat16, jnp.float32
    vm = pl.BlockSpec(memory_space=pltpu.VMEM)
    out = jax.ShapeDtypeStruct((tokens, HD), bf)
    DMA = pltpu.SemaphoreType.DMA
    queries, keys, values, payload, scale = pl.pallas_call(
        functools.partial(body, side, rounds, acts, count, width, kv_heads),
        out_shape=(out, out, out, jax.ShapeDtypeStruct((tokens, width), bf), jax.ShapeDtypeStruct((tokens // 128, 128), f32)),
        in_specs=[pl.BlockSpec(memory_space=pltpu.SMEM), vm, vm, vm, pl.BlockSpec(memory_space=pl.ANY), pl.BlockSpec(memory_space=pl.ANY)],
        out_specs=(vm,) * 5,
        scratch_shapes=[
            pltpu.VMEM((chips, tokens, width), bf),
            pltpu.VMEM((chips, width, HD), bf),
            pltpu.VMEM((chips, width, HD), bf),
            pltpu.VMEM(w_kv.shape, bf),
            pltpu.VMEM(w_kv.shape, bf),
            pltpu.VMEM((2, tokens, HD), f32),
            pltpu.VMEM((2, 2 * KVC, tokens), f32),
            pltpu.VMEM((tokens, HD), f32),
            pltpu.VMEM((2 * KVC, tokens), f32),
            pltpu.VMEM((side, 8, 128), f32),
            pltpu.VMEM((side, 8, 128), f32),
            pltpu.VMEM((8, 128), f32),
            pltpu.VMEM((8, 128), f32),
            pltpu.VMEM((tokens, HD), f32),
            pltpu.VMEM((tokens, HD), f32),
            pltpu.VMEM((2 * KVC, tokens), bf),
            pltpu.VMEM((members, 2 * KVC, tokens), bf),
            DMA((4, most)),
            DMA((4, most)),
            DMA((2,)),
            DMA((3 + 2 * rounds,)),
            DMA((3 + 2 * rounds,)),
            DMA((rounds, members)),
            DMA((rounds, members)),
        ],
        compiler_params=pltpu.CompilerParams(
            collective_id=0, has_side_effects=True, vmem_limit_bytes=62 * 1024 * 1024
        ),
    )(
        prefix,
        hidden,
        norm_gain.reshape(1, width),
        w_scale.reshape(1, -1),
        w_query.reshape(chips, 2, width, HD),
        w_kv,
    )
    return queries, keys, values, payload, scale.reshape(tokens)


def solution(mesh):
    return jax.shard_map(
        functools.partial(local, mesh.shape["tp"]),
        mesh=mesh,
        in_specs=(P("grp", "tp"), P("tp"), P("grp"), P(None, "tp"), P("tp", None), P("tp")),
        out_specs=(P("grp", "tp"), P("grp", "tp"), P("grp", "tp"), P("grp", "tp"), P("grp")),
        check_vma=False,
    )
```

```python
import functools
import heapq
import math

import jax
import jax.numpy as jnp
from jax import lax
from jax.experimental import pallas as pl
from jax.experimental.pallas import tpu as pltpu
from jax.sharding import PartitionSpec as P

HD = 128
KVC = 8
norm_eps = 1e-05
tiny_eps = 1e-06
rope_base = 500000.0

ROUNDS = 1
GROUP = 4
LEAD = 3.0
W_READY = 22.0
STEP = {"R": (0, 1), "L": (0, -1), "U": (1, 0), "D": (-1, 0)}
LINKS = "RLUD"


def plan(side, rounds, unit, lat=1.5):
    half = side // 2

    def signed(v):
        v %= side
        return v - side if v >= half else v

    def onward(kind, dy, dx, via):
        if kind in "SC":
            a, b = (dx, 0) if kind == "S" else (dy, 0)
        else:
            a, b = (dx, dy) if kind == "A" else (dy, dx)
        f1, b1, f2, b2 = ("R", "L", "U", "D") if kind in "AS" else ("U", "D", "R", "L")
        second = [f2, b2] if kind in "AB" else []
        if via is None:
            return [f1, b1] + second
        if b == 0:
            if via == f1 and a > -half:
                return [f1] + second
            if via == b1 and 0 < a < half - 1:
                return [b1] + second
            return second
        if b == -half:
            return []
        if via == f2 and (-b < half - 1 or a < 0):
            return [f2]
        if via == b2 and (b < half - 1 or (b == half - 1 and a >= 0)):
            return [b2]
        return []

    pending = {link: [] for link in LINKS}
    free = {link: 0.0 for link in LINKS}
    count = {link: 0 for link in LINKS}
    actions, heap, tick = [], [], [0]

    def push(time, what):
        tick[0] += 1
        heapq.heappush(heap, (time, tick[0], what))

    def offer(chunk, via, now):
        for link in onward(chunk[0], chunk[2], chunk[3], via):
            tick[0] += 1
            rank = -1 if chunk[0] in "SC" else chunk[1]
            heapq.heappush(pending[link], (rank, tick[0], now, chunk))
            push(now, ("link", link))

    for rnd in range(rounds):
        for kind in "AB":
            offer((kind, rnd, 0, 0), None, 0.0)
    push(0.6, ("stat", "S"))
    left = {"S": side - 1, "C": side - 1}
    arrived = {}
    seen = set()
    while heap:
        now, _, what = heapq.heappop(heap)
        if what[0] == "link":
            link = what[1]
            if not pending[link]:
                continue
            if free[link] > now + 1e-9:
                push(free[link], what)
                continue
            _, _, ready, chunk = heapq.heappop(pending[link])
            took = 0.1 if chunk[0] in "SC" else unit
            free[link] = now + took
            k = count[link]
            count[link] += 1
            actions.append((max(ready, now - LEAD), ("send", link, k, chunk)))
            oy, ox = STEP[link]
            there = (chunk[0], chunk[1], signed(chunk[2] - oy), signed(chunk[3] - ox))
            push(free[link] + lat, ("arrive", link, k, there))
            if pending[link]:
                push(free[link], what)
        elif what[0] == "arrive":
            _, link, k, chunk = what
            assert chunk not in seen
            seen.add(chunk)
            actions.append((now, what))
            offer(chunk, link, now)
            if chunk[0] in "SC":
                left[chunk[0]] -= 1
                if left[chunk[0]] == 0:
                    actions.append((now, ("total", chunk[0])))
                    if chunk[0] == "S":
                        push(now + 0.3, ("stat", "C"))
            else:
                arrived.setdefault((chunk[1], chunk[0]), []).append((now, chunk))
        elif what[0] == "stat":
            offer((what[1], 0, 0, 0), None, now)
    assert len(seen) == 2 * rounds * (side * side - 1) + 2 * (side - 1)
    tasks = []
    for (rnd, kind), got in arrived.items():
        got = [(0.0, (kind, rnd, 0, 0))] + got
        for at in range(0, len(got), GROUP):
            part = got[at : at + GROUP]
            tasks.append((part[-1][0], rnd, ("product", kind, rnd, at == 0, [c[2:] for _, c in part])))
    tasks.sort(key=lambda t: (t[0], t[1]))
    clock = W_READY
    for ready, _, task in tasks:
        clock = max(clock + 0.45, ready)
        actions.append((clock, task))
    last = {}
    for time, what in actions:
        if what[0] == "product":
            last[what[2]] = max(last.get(what[2], 0.0), time)
    end = max(t for t, _ in actions)
    for rnd, time in last.items():
        actions.append((time, ("partial", rnd)))
        actions.append((time + 1.8 if time < end - 3 else end + 1, ("share", rnd)))
    order = sorted(range(len(actions)), key=lambda i: (actions[i][0], i))
    return [actions[i][1] for i in order], count


def swap_pairs(x, axis):
    size = x.shape[axis]
    even = lax.broadcasted_iota(jnp.int32, x.shape, axis) % 2 == 0
    return jnp.where(even, pltpu.roll(x, size - 1, axis), pltpu.roll(x, 1, axis))


def frequency(columns):
    index = ((columns % HD) // 2).astype(jnp.float32)
    return jnp.exp2(index * (-2.0 * math.log2(rope_base) / HD))


def body(
    side, rounds, acts, count, width, kv_heads,
    prefix, h_in, g_in, ws_in, wq_ref, wkv_ref,
    q_out, p_out, heads, both_out,
    h_ref, g_ref, ws_ref, xs, w_own, w_oth, kv_own, kv_oth, acc_q, acc_kv, part_q, part_kv,
    stat_row, stat_col, stat_oth, stat_t, cos_q, sin_q, share,
    send_sem, recv_sem, local_sem, pair_send, pair_recv, share_send, share_recv,
):
    tokens = h_in.shape[0]
    blocks = tokens // 128
    span = tokens // rounds
    half = span // 2
    me = lax.axis_index("tp")
    core = me % 2
    x = (me // 2) % side
    y = me // (2 * side)
    MESH = pl.DeviceIdType.MESH

    def device(yy, xx, cc):
        return {"tp": (yy * side + xx) * 2 + cc}

    partner = device(y, x, 1 - core)

    def slot_of(dy, dx):
        return ((y + dy + side) % side) * side + (x + dx + side) % side

    near = {
        link: device((y + oy + side) % side, (x + ox + side) % side, core)
        for link, (oy, ox) in STEP.items()
    }
    barrier = pltpu.get_barrier_semaphore()
    for target in near.values():
        pl.semaphore_signal(barrier, inc=1, device_id=target, device_id_type=MESH)
    ins = [
        pltpu.make_async_copy(a, b, local_sem.at[2 + i])
        for i, (a, b) in enumerate([(h_in, h_ref), (g_in, g_ref), (ws_in, ws_ref)])
    ]
    for copy in ins:
        copy.start()

    own_w = pltpu.make_async_copy(wq_ref.at[:, core], w_own, local_sem.at[0])
    own_kv = pltpu.make_async_copy(wkv_ref, kv_own, local_sem.at[1])
    own_w.start()
    own_kv.start()

    for copy in ins:
        copy.wait()
    gain = g_ref[...]
    mine = slot_of(0, 0)
    for b in range(blocks):
        rows = slice(b * 128, (b + 1) * 128)
        xs[mine, rows, :] = (h_ref[rows, :].astype(jnp.float32) * gain).astype(jnp.bfloat16)

    @pl.when(core == 1)
    def _():
        pl.semaphore_wait(barrier, 4)

    @pl.when(core == 0)
    def _():
        pl.semaphore_wait(barrier, 5)

    pl.semaphore_signal(barrier, inc=1, device_id=partner, device_id_type=MESH)

    def remote(src, dst, ssem, rsem, target):
        return pltpu.make_async_remote_copy(
            src_ref=src, dst_ref=dst, send_sem=ssem, recv_sem=rsem, device_id=target, device_id_type=MESH
        )

    give_kv = remote(wkv_ref, kv_oth, pair_send.at[0], pair_recv.at[0], partner)
    give_w = remote(wq_ref.at[:, 1 - core], w_oth, pair_send.at[1], pair_recv.at[1], partner)

    def tokens_of(kind, rnd):
        return rnd * span + (half if kind == "B" else 0)

    def place(chunk):
        kind, rnd, dy, dx = chunk
        if kind == "S":
            return stat_row.at[(x + dx + side) % side]
        if kind == "C":
            return stat_col.at[(y + dy + side) % side]
        return xs.at[slot_of(dy, dx), pl.ds(tokens_of(kind, rnd), half), :]

    def hop(link, k, chunk):
        ref = place(chunk)
        return remote(ref, ref, send_sem.at[LINKS.index(link), k], recv_sem.at[LINKS.index(link), k], near[link])

    def statistics():
        lane = lax.broadcasted_iota(jnp.int32, (128, 128), 1)
        total = jnp.zeros((128, 128), jnp.float32)
        for b in range(blocks):
            rows = slice(b * 128, (b + 1) * 128)
            wide = h_ref[rows, :].astype(jnp.float32)
            squares = jnp.sum(wide * wide, axis=1, keepdims=True)
            peak = jnp.max(jnp.abs(wide * gain), axis=1, keepdims=True)
            total = jnp.where(lane == 2 * b, squares, total)
            total = jnp.where(lane == 2 * b + 1, peak, total)
        stat_row[x] = jnp.transpose(total)[:8]

    def joined(a, b):
        even = lax.broadcasted_iota(jnp.int32, (8, 128), 0) % 2 == 0
        return jnp.where(even, a + b, jnp.maximum(a, b))

    def angles(b):
        rows = slice(b * 128, (b + 1) * 128)
        pos = prefix[0] + b * 128 + lax.broadcasted_iota(jnp.int32, (128, 128), 0)
        col = lax.broadcasted_iota(jnp.int32, (128, 128), 1)
        angle = pos.astype(jnp.float32) * frequency(col)
        sine = jnp.sin(angle)
        cos_q[rows, :] = jnp.cos(angle)
        sin_q[rows, :] = jnp.where(col % 2 == 0, -sine, sine)

    def product(kind, rnd, first, places):
        t0 = tokens_of(kind, rnd)
        slots = [slot_of(*p) for p in places]
        left = jnp.concatenate([xs[s, t0 : t0 + half, :] for s in slots], axis=1)
        right = jnp.concatenate([jnp.concatenate([w_own[s], w_oth[s]], axis=1) for s in slots], axis=0)
        out = jnp.dot(left, right, preferred_element_type=jnp.float32)
        starts = [pl.multiple_of((s * 2 + core) * width, width) for s in slots]
        rows_kv = jnp.concatenate(
            [jnp.concatenate([r[:, pl.ds(c, width)] for c in starts], axis=1) for r in (kv_own, kv_oth)], axis=0
        )
        kv = lax.dot_general(rows_kv, left, (((1,), (1,)), ((), ())), preferred_element_type=jnp.float32)
        for who in range(2):
            piece = out[:, who * HD : (who + 1) * HD]
            kvp = kv[who * 2 * KVC : (who + 1) * 2 * KVC]
            if first:
                acc_q[who, t0 : t0 + half, :] = piece
                acc_kv[who, :, t0 : t0 + half] = kvp
            else:
                acc_q[who, t0 : t0 + half, :] += piece
                acc_kv[who, :, t0 : t0 + half] += kvp

    def pair_copy(rnd, what):
        rng = pl.ds(rnd * span, span)
        if what == "kv":
            return remote(
                acc_kv.at[1, :, rng], part_kv.at[:, rng], pair_send.at[2 + rnd], pair_recv.at[2 + rnd], partner
            )
        at = 2 + rounds + rnd
        return remote(acc_q.at[1, rng, :], part_q.at[rng, :], pair_send.at[at], pair_recv.at[at], partner)

    give_stat = remote(
        stat_t, stat_oth, pair_send.at[2 + 2 * rounds], pair_recv.at[2 + 2 * rounds], partner
    )

    piece_me = me // kv_heads
    members = 2 * side * side // kv_heads
    head_to = me % kv_heads
    head_me = me // members

    def share_copy(rnd, m):
        rng = pl.ds(rnd * span, span)
        target = head_to * members + (m + me) % members
        return target, remote(
            share.at[:, rng], heads.at[piece_me, :, rng], share_send.at[rnd, m], share_recv.at[rnd, piece_me],
            {"tp": target},
        )

    ws_row = ws_ref[:, :HD]

    def share_round(rnd):
        rng = slice(rnd * span, (rnd + 1) * span)
        pair_copy(rnd, "kv").wait_recv()
        eye = lax.broadcasted_iota(jnp.int32, (2 * KVC, 2 * KVC), 0) == lax.broadcasted_iota(
            jnp.int32, (2 * KVC, 2 * KVC), 1
        )
        ws_col = jnp.sum(jnp.where(eye, ws_ref[:, HD:], 0.0), axis=1, keepdims=True)
        kv = (acc_kv[0, :, rng] + part_kv[:, rng]) * ws_col
        key, value = kv[:KVC], kv[KVC:]
        pos = prefix[0] + rnd * span + lax.broadcasted_iota(jnp.int32, (KVC, span), 1)
        row = lax.broadcasted_iota(jnp.int32, (KVC, span), 0)
        angle = pos.astype(jnp.float32) * frequency(piece_me * KVC + row)
        sine = jnp.sin(angle)
        key = key * jnp.cos(angle) + swap_pairs(key, 0) * jnp.where(row % 2 == 0, -sine, sine)
        both = jnp.concatenate([key, value], axis=0).astype(jnp.bfloat16)
        share[:, rng] = both

        @pl.when(head_to == head_me)
        def _():
            heads[piece_me, :, rng] = both

        for m in range(members):
            target, copy = share_copy(rnd, m)

            @pl.when(target != me)
            def _():
                copy.start()

    @pl.when(core == 0)
    def _():
        give_kv.start()
        give_w.start()

    started = weighed = False
    for act in acts:
        if act[0] == "send":
            _, link, k, chunk = act
            if chunk[0] == "S" and not started:
                started = True
                statistics()
            hop(link, k, chunk).start()
        elif act[0] == "arrive":
            _, link, k, chunk = act
            hop(link, k, chunk).wait_recv()
        elif act[0] == "total":
            if act[1] == "S":
                total = stat_row[0]
                for i in range(1, side):
                    total = joined(total, stat_row[i])
                stat_col[y] = total
                for b in range(blocks):
                    angles(b)
            else:
                total = stat_col[0]
                for i in range(1, side):
                    total = joined(total, stat_col[i])
                stat_t[...] = total
                give_stat.start()
        elif act[0] == "product":
            if not weighed:
                weighed = True
                own_w.wait()
                own_kv.wait()

                @pl.when(core == 1)
                def _():
                    pl.semaphore_wait(barrier, 1)
                    give_kv.start()
                    give_w.start()

                give_kv.wait_recv()
                give_w.wait_recv()
            product(*act[1:])
        elif act[0] == "partial":
            pair_copy(act[1], "kv").start()
            pair_copy(act[1], "q").start()
        elif act[0] == "share":
            share_round(act[1])

    give_stat.wait_recv()
    total = joined(stat_t[...], stat_oth[...])
    inverse = 1.0 / jnp.sqrt(total / (width * 2 * side * side) + norm_eps)
    even = lax.broadcasted_iota(jnp.int32, (8, 128), 0) % 2 == 0
    both = jnp.where(even, inverse, total * pltpu.roll(inverse, 1, 0) + tiny_eps)
    both_out[...] = both
    columns = jnp.transpose(jnp.concatenate([both, jnp.zeros((120, 128), jnp.float32)], axis=0))
    inv = [columns[:, 2 * b : 2 * b + 1] for b in range(blocks)]
    for b in range(blocks):
        rows = slice(b * 128, (b + 1) * 128)
        weighted = h_ref[rows, :].astype(jnp.float32) * gain
        p_out[rows, :] = ((weighted * inv[b]) / columns[:, 2 * b + 1 : 2 * b + 2]).astype(jnp.bfloat16)

    for rnd in range(rounds):
        pair_copy(rnd, "q").wait_recv()
    for b in range(blocks):
        rows = slice(b * 128, (b + 1) * 128)
        q = (acc_q[0, rows, :] + part_q[rows, :]) * ws_row * inv[b]
        q_out[rows, :] = (q * cos_q[rows, :] + swap_pairs(q, 1) * sin_q[rows, :]).astype(jnp.bfloat16)

    for rnd in range(rounds):
        for p in range(members):
            source = p * kv_heads + head_me
            rng = pl.ds(rnd * span, span)

            @pl.when(source != me)
            def _():
                remote(
                    heads.at[p, :, rng], heads.at[p, :, rng], share_send.at[rnd, 0], share_recv.at[rnd, p], partner
                ).wait_recv()

    for act in acts:
        if act[0] == "send":
            hop(*act[1:]).wait_send()
    give_kv.wait_send()
    give_w.wait_send()
    give_stat.wait_send()
    for rnd in range(rounds):
        pair_copy(rnd, "kv").wait_send()
        pair_copy(rnd, "q").wait_send()
        for m in range(members):
            target, copy = share_copy(rnd, m)

            @pl.when(target != me)
            def _():
                copy.wait_send()


def finish(blocks, members, q_in, p_in, heads, both, q_out, k_out, v_out, p_out, rs_out):
    q_out[...] = q_in[...]
    p_out[...] = p_in[...]
    both = both[...]
    rs_out[...] = jnp.concatenate([both[2 * b + 1 : 2 * b + 2] for b in range(blocks)], axis=0)
    for b in range(blocks):
        rows = slice(b * 128, (b + 1) * 128)
        got = [heads[p, :, rows].astype(jnp.float32) for p in range(members)]
        inverse = both[2 * b : 2 * b + 1]
        for out, at in ((k_out, 0), (v_out, KVC)):
            turned = jnp.concatenate([g[at : at + KVC] for g in got], axis=0) * inverse
            out[rows, :] = jnp.transpose(turned).astype(jnp.bfloat16)


def local(tp, hidden, norm_gain, prefix, w_query, w_kv, w_scale):
    tokens, width = hidden.shape
    side = math.isqrt(tp // 2)
    kv_heads = KVC * tp // HD
    members = tp // kv_heads
    rounds = ROUNDS
    acts, count = plan(side, rounds, 1.41 / rounds, 2.0)
    most = max(count.values())
    chips = tp // 2
    bf, f32 = jnp.bfloat16, jnp.float32
    vm = pl.BlockSpec(memory_space=pltpu.VMEM)
    out = jax.ShapeDtypeStruct((tokens, HD), bf)
    DMA = pltpu.SemaphoreType.DMA
    hbm = pl.BlockSpec(memory_space=pltpu.HBM)
    out_p = jax.ShapeDtypeStruct((tokens, width), bf)
    queries, payload, heads, both = pl.pallas_call(
        functools.partial(body, side, rounds, acts, count, width, kv_heads),
        out_shape=(out, out_p, jax.ShapeDtypeStruct((members, 2 * KVC, tokens), bf), jax.ShapeDtypeStruct((8, 128), f32)),
        in_specs=[pl.BlockSpec(memory_space=pltpu.SMEM)] + [hbm] * 5,
        out_specs=(vm,) * 4,
        scratch_shapes=[
            pltpu.VMEM((tokens, width), bf),
            pltpu.VMEM((1, width), f32),
            pltpu.VMEM((1, w_scale.shape[0]), f32),
            pltpu.VMEM((chips, tokens, width), bf),
            pltpu.VMEM((chips, width, HD), bf),
            pltpu.VMEM((chips, width, HD), bf),
            pltpu.VMEM(w_kv.shape, bf),
            pltpu.VMEM(w_kv.shape, bf),
            pltpu.VMEM((2, tokens, HD), f32),
            pltpu.VMEM((2, 2 * KVC, tokens), f32),
            pltpu.VMEM((tokens, HD), f32),
            pltpu.VMEM((2 * KVC, tokens), f32),
            pltpu.VMEM((side, 8, 128), f32),
            pltpu.VMEM((side, 8, 128), f32),
            pltpu.VMEM((8, 128), f32),
            pltpu.VMEM((8, 128), f32),
            pltpu.VMEM((tokens, HD), f32),
            pltpu.VMEM((tokens, HD), f32),
            pltpu.VMEM((2 * KVC, tokens), bf),
            DMA((4, most)),
            DMA((4, most)),
            DMA((6,)),
            DMA((3 + 2 * rounds,)),
            DMA((3 + 2 * rounds,)),
            DMA((rounds, members)),
            DMA((rounds, members)),
        ],
        compiler_params=pltpu.CompilerParams(
            collective_id=0, has_side_effects=True, vmem_limit_bytes=24 * 1024 * 1024
        ),
    )(
        prefix,
        *(
            pltpu.with_memory_space_constraint(a, pltpu.HBM)
            for a in (
                hidden,
                norm_gain.reshape(1, width),
                w_scale.reshape(1, -1),
                w_query.reshape(chips, 2, width, HD),
                w_kv,
            )
        )
    )
    queries, keys, values, payload, scale = pl.pallas_call(
        functools.partial(finish, tokens // 128, members),
        out_shape=(out, out, out, out_p, jax.ShapeDtypeStruct((tokens // 128, 128), f32)),
        in_specs=[vm] * 4,
        out_specs=(vm,) * 5,
        compiler_params=pltpu.CompilerParams(vmem_limit_bytes=8 * 1024 * 1024),
    )(queries, payload, heads, both)
    return queries, keys, values, payload, scale.reshape(tokens)


def solution(mesh):
    return jax.shard_map(
        functools.partial(local, mesh.shape["tp"]),
        mesh=mesh,
        in_specs=(P("grp", "tp"), P("tp"), P("grp"), P(None, "tp"), P("tp", None), P("tp")),
        out_specs=(P("grp", "tp"), P("grp", "tp"), P("grp", "tp"), P("grp", "tp"), P("grp")),
        check_vma=False,
    )
```

```python
import functools
import heapq
import math

import jax
import jax.numpy as jnp
from jax import lax
from jax.experimental import pallas as pl
from jax.experimental.pallas import tpu as pltpu
from jax.sharding import PartitionSpec as P

HD = 128
KVC = 8
norm_eps = 1e-05
tiny_eps = 1e-06
rope_base = 500000.0

ROUNDS = 1
GROUP = 4
LEAD = 6.0
W_READY = 28.0
STEP = {"R": (0, 1), "L": (0, -1), "U": (1, 0), "D": (-1, 0)}
LINKS = "RLUD"


def plan(side, rounds, unit, lat=3.5):
    half = side // 2

    def signed(v):
        v %= side
        return v - side if v >= half else v

    def onward(kind, dy, dx, via):
        if kind in "SC":
            a, b = (dx, 0) if kind == "S" else (dy, 0)
        else:
            a, b = (dx, dy) if kind == "A" else (dy, dx)
        f1, b1, f2, b2 = ("R", "L", "U", "D") if kind in "AS" else ("U", "D", "R", "L")
        second = [f2, b2] if kind in "AB" else []
        if via is None:
            return [f1, b1] + second
        if b == 0:
            if via == f1 and a > -half:
                return [f1] + second
            if via == b1 and 0 < a < half - 1:
                return [b1] + second
            return second
        if b == -half:
            return []
        if via == f2 and (-b < half - 1 or a < 0):
            return [f2]
        if via == b2 and (b < half - 1 or (b == half - 1 and a >= 0)):
            return [b2]
        return []

    pending = {link: [] for link in LINKS}
    free = {link: 0.0 for link in LINKS}
    count = {link: 0 for link in LINKS}
    actions, heap, tick = [], [], [0]

    def push(time, what):
        tick[0] += 1
        heapq.heappush(heap, (time, tick[0], what))

    def offer(chunk, via, now):
        for link in onward(chunk[0], chunk[2], chunk[3], via):
            tick[0] += 1
            rank = -1 if chunk[0] in "SC" else abs(chunk[2] if chunk[0] == "A" else chunk[3])
            heapq.heappush(pending[link], (rank, tick[0], now, chunk))
            push(now, ("link", link))

    for rnd in range(rounds):
        for kind in "AB":
            offer((kind, rnd, 0, 0), None, 0.0)
    push(0.6, ("stat", "S"))
    left = {"S": side - 1, "C": side - 1}
    arrived = {}
    seen = set()
    while heap:
        now, _, what = heapq.heappop(heap)
        if what[0] == "link":
            link = what[1]
            if not pending[link]:
                continue
            if free[link] > now + 1e-9:
                push(free[link], what)
                continue
            _, _, ready, chunk = heapq.heappop(pending[link])
            took = 0.1 if chunk[0] in "SC" else unit
            free[link] = now + took
            k = count[link]
            count[link] += 1
            actions.append((max(ready, now - LEAD), ("send", link, k, chunk)))
            oy, ox = STEP[link]
            there = (chunk[0], chunk[1], signed(chunk[2] - oy), signed(chunk[3] - ox))
            push(free[link] + lat, ("arrive", link, k, there))
            if pending[link]:
                push(free[link], what)
        elif what[0] == "arrive":
            _, link, k, chunk = what
            assert chunk not in seen
            seen.add(chunk)
            actions.append((now, what))
            offer(chunk, link, now)
            if chunk[0] in "SC":
                left[chunk[0]] -= 1
                if left[chunk[0]] == 0:
                    actions.append((now, ("total", chunk[0])))
                    if chunk[0] == "S":
                        push(now + 0.3, ("stat", "C"))
            else:
                arrived.setdefault((chunk[1], chunk[0]), []).append((now, chunk))
        elif what[0] == "stat":
            offer((what[1], 0, 0, 0), None, now)
    assert len(seen) == 2 * rounds * (side * side - 1) + 2 * (side - 1)
    tasks = []
    for (rnd, kind), got in arrived.items():
        got = [(0.0, (kind, rnd, 0, 0))] + got
        for at in range(0, len(got), GROUP):
            part = got[at : at + GROUP]
            tasks.append((part[-1][0], rnd, ("product", kind, rnd, at == 0, [c[2:] for _, c in part])))
    tasks.sort(key=lambda t: (t[0], t[1]))
    clock = W_READY
    for ready, _, task in tasks:
        clock = max(clock + 0.45, ready)
        actions.append((clock, task))
    last = {}
    for time, what in actions:
        if what[0] == "product":
            last[what[2]] = max(last.get(what[2], 0.0), time)
    end = max(t for t, _ in actions)
    for rnd, time in last.items():
        actions.append((time, ("partial", rnd)))
        actions.append((time + 1.8 if time < end - 3 else end + 1, ("share", rnd)))
    order = sorted(range(len(actions)), key=lambda i: (actions[i][0], i))
    return [actions[i][1] for i in order], count


def swap_pairs(x, axis):
    size = x.shape[axis]
    even = lax.broadcasted_iota(jnp.int32, x.shape, axis) % 2 == 0
    return jnp.where(even, pltpu.roll(x, size - 1, axis), pltpu.roll(x, 1, axis))


def frequency(columns):
    index = ((columns % HD) // 2).astype(jnp.float32)
    return jnp.exp2(index * (-2.0 * math.log2(rope_base) / HD))


def body(
    side, rounds, acts, count, width, kv_heads,
    prefix, h_in, g_in, ws_in, wq_ref, wkv_ref,
    q_out, p_out, heads, both_out,
    h_ref, g_ref, ws_ref, xs, w_own, w_oth, kv_own, kv_oth, acc_q, acc_kv, part_q, part_kv,
    stat_row, stat_col, stat_oth, stat_t, cos_q, sin_q, share,
    send_sem, recv_sem, local_sem, pair_send, pair_recv, share_send, share_recv,
):
    tokens = h_in.shape[0]
    blocks = tokens // 128
    span = tokens // rounds
    half = span // 2
    me = lax.axis_index("tp")
    core = me % 2
    x = (me // 2) % side
    y = me // (2 * side)
    MESH = pl.DeviceIdType.MESH

    def device(yy, xx, cc):
        return {"tp": (yy * side + xx) * 2 + cc}

    partner = device(y, x, 1 - core)

    def slot_of(dy, dx):
        return ((y + dy + side) % side) * side + (x + dx + side) % side

    near = {
        link: device((y + oy + side) % side, (x + ox + side) % side, core)
        for link, (oy, ox) in STEP.items()
    }
    barrier = pltpu.get_barrier_semaphore()
    for target in near.values():
        pl.semaphore_signal(barrier, inc=1, device_id=target, device_id_type=MESH)
    ins = [
        pltpu.make_async_copy(a, b, local_sem.at[2 + i])
        for i, (a, b) in enumerate([(h_in, h_ref), (g_in, g_ref), (ws_in, ws_ref)])
    ]
    for copy in ins:
        copy.start()

    own_w = pltpu.make_async_copy(wq_ref.at[:, core], w_own, local_sem.at[0])
    own_kv = pltpu.make_async_copy(wkv_ref, kv_own, local_sem.at[1])
    own_w.start()
    own_kv.start()

    for copy in ins:
        copy.wait()
    gain = g_ref[...]
    mine = slot_of(0, 0)
    for b in range(blocks):
        rows = slice(b * 128, (b + 1) * 128)
        xs[mine, rows, :] = (h_ref[rows, :].astype(jnp.float32) * gain).astype(jnp.bfloat16)

    @pl.when(core == 1)
    def _():
        pl.semaphore_wait(barrier, 4)

    @pl.when(core == 0)
    def _():
        pl.semaphore_wait(barrier, 5)

    pl.semaphore_signal(barrier, inc=1, device_id=partner, device_id_type=MESH)

    def remote(src, dst, ssem, rsem, target):
        return pltpu.make_async_remote_copy(
            src_ref=src, dst_ref=dst, send_sem=ssem, recv_sem=rsem, device_id=target, device_id_type=MESH
        )

    give_kv = remote(wkv_ref, kv_oth, pair_send.at[0], pair_recv.at[0], partner)
    give_w = remote(wq_ref.at[:, 1 - core], w_oth, pair_send.at[1], pair_recv.at[1], partner)

    def tokens_of(kind, rnd):
        return rnd * span + (half if kind == "B" else 0)

    def place(chunk):
        kind, rnd, dy, dx = chunk
        if kind == "S":
            return stat_row.at[(x + dx + side) % side]
        if kind == "C":
            return stat_col.at[(y + dy + side) % side]
        return xs.at[slot_of(dy, dx), pl.ds(tokens_of(kind, rnd), half), :]

    def hop(link, k, chunk):
        ref = place(chunk)
        return remote(ref, ref, send_sem.at[LINKS.index(link), k], recv_sem.at[LINKS.index(link), k], near[link])

    def statistics():
        lane = lax.broadcasted_iota(jnp.int32, (128, 128), 1)
        total = jnp.zeros((128, 128), jnp.float32)
        for b in range(blocks):
            rows = slice(b * 128, (b + 1) * 128)
            wide = h_ref[rows, :].astype(jnp.float32)
            squares = jnp.sum(wide * wide, axis=1, keepdims=True)
            peak = jnp.max(jnp.abs(wide * gain), axis=1, keepdims=True)
            total = jnp.where(lane == 2 * b, squares, total)
            total = jnp.where(lane == 2 * b + 1, peak, total)
        stat_row[x] = jnp.transpose(total)[:8]

    def joined(a, b):
        even = lax.broadcasted_iota(jnp.int32, (8, 128), 0) % 2 == 0
        return jnp.where(even, a + b, jnp.maximum(a, b))

    def angles(b):
        rows = slice(b * 128, (b + 1) * 128)
        pos = prefix[0] + b * 128 + lax.broadcasted_iota(jnp.int32, (128, 128), 0)
        col = lax.broadcasted_iota(jnp.int32, (128, 128), 1)
        angle = pos.astype(jnp.float32) * frequency(col)
        sine = jnp.sin(angle)
        cos_q[rows, :] = jnp.cos(angle)
        sin_q[rows, :] = jnp.where(col % 2 == 0, -sine, sine)

    def product(kind, rnd, first, places):
        t0 = tokens_of(kind, rnd)
        slots = [slot_of(*p) for p in places]
        left = jnp.concatenate([xs[s, t0 : t0 + half, :] for s in slots], axis=1)
        right = jnp.concatenate([jnp.concatenate([w_own[s], w_oth[s]], axis=1) for s in slots], axis=0)
        out = jnp.dot(left, right, preferred_element_type=jnp.float32)
        starts = [pl.multiple_of((s * 2 + core) * width, width) for s in slots]
        rows_kv = jnp.concatenate(
            [jnp.concatenate([r[:, pl.ds(c, width)] for c in starts], axis=1) for r in (kv_own, kv_oth)], axis=0
        )
        kv = lax.dot_general(rows_kv, left, (((1,), (1,)), ((), ())), preferred_element_type=jnp.float32)
        for who in range(2):
            piece = out[:, who * HD : (who + 1) * HD]
            kvp = kv[who * 2 * KVC : (who + 1) * 2 * KVC]
            if first:
                acc_q[who, t0 : t0 + half, :] = piece
                acc_kv[who, :, t0 : t0 + half] = kvp
            else:
                acc_q[who, t0 : t0 + half, :] += piece
                acc_kv[who, :, t0 : t0 + half] += kvp

    def pair_copy(rnd, what):
        rng = pl.ds(rnd * span, span)
        if what == "kv":
            return remote(
                acc_kv.at[1, :, rng], part_kv.at[:, rng], pair_send.at[2 + rnd], pair_recv.at[2 + rnd], partner
            )
        at = 2 + rounds + rnd
        return remote(acc_q.at[1, rng, :], part_q.at[rng, :], pair_send.at[at], pair_recv.at[at], partner)

    give_stat = remote(
        stat_t, stat_oth, pair_send.at[2 + 2 * rounds], pair_recv.at[2 + 2 * rounds], partner
    )

    piece_me = me // kv_heads
    members = 2 * side * side // kv_heads
    head_to = me % kv_heads
    head_me = me // members

    def share_copy(rnd, m):
        rng = pl.ds(rnd * span, span)
        target = head_to * members + (m + me) % members
        return target, remote(
            share.at[:, rng], heads.at[piece_me, :, rng], share_send.at[rnd, m], share_recv.at[rnd, piece_me],
            {"tp": target},
        )

    ws_row = ws_ref[:, :HD]

    def share_round(rnd):
        rng = slice(rnd * span, (rnd + 1) * span)
        pair_copy(rnd, "kv").wait_recv()
        eye = lax.broadcasted_iota(jnp.int32, (2 * KVC, 2 * KVC), 0) == lax.broadcasted_iota(
            jnp.int32, (2 * KVC, 2 * KVC), 1
        )
        ws_col = jnp.sum(jnp.where(eye, ws_ref[:, HD:], 0.0), axis=1, keepdims=True)
        kv = (acc_kv[0, :, rng] + part_kv[:, rng]) * ws_col
        key, value = kv[:KVC], kv[KVC:]
        pos = prefix[0] + rnd * span + lax.broadcasted_iota(jnp.int32, (KVC, span), 1)
        row = lax.broadcasted_iota(jnp.int32, (KVC, span), 0)
        angle = pos.astype(jnp.float32) * frequency(piece_me * KVC + row)
        sine = jnp.sin(angle)
        key = key * jnp.cos(angle) + swap_pairs(key, 0) * jnp.where(row % 2 == 0, -sine, sine)
        both = jnp.concatenate([key, value], axis=0).astype(jnp.bfloat16)
        share[:, rng] = both

        @pl.when(head_to == head_me)
        def _():
            heads[piece_me, :, rng] = both

        for m in range(members):
            target, copy = share_copy(rnd, m)

            @pl.when(target != me)
            def _():
                copy.start()

    @pl.when(core == 0)
    def _():
        give_kv.start()
        give_w.start()

    started = weighed = False
    for act in acts:
        if act[0] == "send":
            _, link, k, chunk = act
            if chunk[0] == "S" and not started:
                started = True
                statistics()
            hop(link, k, chunk).start()
        elif act[0] == "arrive":
            _, link, k, chunk = act
            hop(link, k, chunk).wait_recv()
        elif act[0] == "total":
            if act[1] == "S":
                total = stat_row[0]
                for i in range(1, side):
                    total = joined(total, stat_row[i])
                stat_col[y] = total
                for b in range(blocks):
                    angles(b)
            else:
                total = stat_col[0]
                for i in range(1, side):
                    total = joined(total, stat_col[i])
                stat_t[...] = total
                give_stat.start()
        elif act[0] == "product":
            if not weighed:
                weighed = True
                own_w.wait()
                own_kv.wait()

                @pl.when(core == 1)
                def _():
                    pl.semaphore_wait(barrier, 1)
                    give_kv.start()
                    give_w.start()

                give_kv.wait_recv()
                give_w.wait_recv()
            product(*act[1:])
        elif act[0] == "partial":
            pair_copy(act[1], "kv").start()
            pair_copy(act[1], "q").start()
        elif act[0] == "share":
            share_round(act[1])

    give_stat.wait_recv()
    total = joined(stat_t[...], stat_oth[...])
    inverse = 1.0 / jnp.sqrt(total / (width * 2 * side * side) + norm_eps)
    even = lax.broadcasted_iota(jnp.int32, (8, 128), 0) % 2 == 0
    both = jnp.where(even, inverse, total * pltpu.roll(inverse, 1, 0) + tiny_eps)
    both_out[...] = both
    columns = jnp.transpose(jnp.concatenate([both, jnp.zeros((120, 128), jnp.float32)], axis=0))
    inv = [columns[:, 2 * b : 2 * b + 1] for b in range(blocks)]
    for b in range(blocks):
        rows = slice(b * 128, (b + 1) * 128)
        weighted = h_ref[rows, :].astype(jnp.float32) * gain
        p_out[rows, :] = ((weighted * inv[b]) / columns[:, 2 * b + 1 : 2 * b + 2]).astype(jnp.bfloat16)

    for rnd in range(rounds):
        pair_copy(rnd, "q").wait_recv()
    for b in range(blocks):
        rows = slice(b * 128, (b + 1) * 128)
        q = (acc_q[0, rows, :] + part_q[rows, :]) * ws_row * inv[b]
        q_out[rows, :] = (q * cos_q[rows, :] + swap_pairs(q, 1) * sin_q[rows, :]).astype(jnp.bfloat16)

    for rnd in range(rounds):
        for p in range(members):
            source = p * kv_heads + head_me
            rng = pl.ds(rnd * span, span)

            @pl.when(source != me)
            def _():
                remote(
                    heads.at[p, :, rng], heads.at[p, :, rng], share_send.at[rnd, 0], share_recv.at[rnd, p], partner
                ).wait_recv()

    for act in acts:
        if act[0] == "send":
            hop(*act[1:]).wait_send()
    give_kv.wait_send()
    give_w.wait_send()
    give_stat.wait_send()
    for rnd in range(rounds):
        pair_copy(rnd, "kv").wait_send()
        pair_copy(rnd, "q").wait_send()
        for m in range(members):
            target, copy = share_copy(rnd, m)

            @pl.when(target != me)
            def _():
                copy.wait_send()


def finish(blocks, members, q_in, p_in, heads, both, q_out, k_out, v_out, p_out, rs_out):
    q_out[...] = q_in[...]
    p_out[...] = p_in[...]
    both = both[...]
    rs_out[...] = jnp.concatenate([both[2 * b + 1 : 2 * b + 2] for b in range(blocks)], axis=0)
    for b in range(blocks):
        rows = slice(b * 128, (b + 1) * 128)
        got = [heads[p, :, rows].astype(jnp.float32) for p in range(members)]
        inverse = both[2 * b : 2 * b + 1]
        for out, at in ((k_out, 0), (v_out, KVC)):
            turned = jnp.concatenate([g[at : at + KVC] for g in got], axis=0) * inverse
            out[rows, :] = jnp.transpose(turned).astype(jnp.bfloat16)


def local(tp, hidden, norm_gain, prefix, w_query, w_kv, w_scale):
    tokens, width = hidden.shape
    side = math.isqrt(tp // 2)
    kv_heads = KVC * tp // HD
    members = tp // kv_heads
    rounds = ROUNDS
    acts, count = plan(side, rounds, 1.41 / rounds)
    most = max(count.values())
    chips = tp // 2
    bf, f32 = jnp.bfloat16, jnp.float32
    vm = pl.BlockSpec(memory_space=pltpu.VMEM)
    out = jax.ShapeDtypeStruct((tokens, HD), bf)
    DMA = pltpu.SemaphoreType.DMA
    hbm = pl.BlockSpec(memory_space=pltpu.HBM)
    out_p = jax.ShapeDtypeStruct((tokens, width), bf)
    queries, payload, heads, both = pl.pallas_call(
        functools.partial(body, side, rounds, acts, count, width, kv_heads),
        out_shape=(out, out_p, jax.ShapeDtypeStruct((members, 2 * KVC, tokens), bf), jax.ShapeDtypeStruct((8, 128), f32)),
        in_specs=[pl.BlockSpec(memory_space=pltpu.SMEM)] + [hbm] * 5,
        out_specs=(vm,) * 4,
        scratch_shapes=[
            pltpu.VMEM((tokens, width), bf),
            pltpu.VMEM((1, width), f32),
            pltpu.VMEM((1, w_scale.shape[0]), f32),
            pltpu.VMEM((chips, tokens, width), bf),
            pltpu.VMEM((chips, width, HD), bf),
            pltpu.VMEM((chips, width, HD), bf),
            pltpu.VMEM(w_kv.shape, bf),
            pltpu.VMEM(w_kv.shape, bf),
            pltpu.VMEM((2, tokens, HD), f32),
            pltpu.VMEM((2, 2 * KVC, tokens), f32),
            pltpu.VMEM((tokens, HD), f32),
            pltpu.VMEM((2 * KVC, tokens), f32),
            pltpu.VMEM((side, 8, 128), f32),
            pltpu.VMEM((side, 8, 128), f32),
            pltpu.VMEM((8, 128), f32),
            pltpu.VMEM((8, 128), f32),
            pltpu.VMEM((tokens, HD), f32),
            pltpu.VMEM((tokens, HD), f32),
            pltpu.VMEM((2 * KVC, tokens), bf),
            DMA((4, most)),
            DMA((4, most)),
            DMA((6,)),
            DMA((3 + 2 * rounds,)),
            DMA((3 + 2 * rounds,)),
            DMA((rounds, members)),
            DMA((rounds, members)),
        ],
        compiler_params=pltpu.CompilerParams(
            collective_id=0, has_side_effects=True, vmem_limit_bytes=24 * 1024 * 1024
        ),
    )(
        prefix,
        *(
            pltpu.with_memory_space_constraint(a, pltpu.HBM)
            for a in (
                hidden,
                norm_gain.reshape(1, width),
                w_scale.reshape(1, -1),
                w_query.reshape(chips, 2, width, HD),
                w_kv,
            )
        )
    )
    queries, keys, values, payload, scale = pl.pallas_call(
        functools.partial(finish, tokens // 128, members),
        out_shape=(out, out, out, out_p, jax.ShapeDtypeStruct((tokens // 128, 128), f32)),
        in_specs=[vm] * 4,
        out_specs=(vm,) * 5,
        compiler_params=pltpu.CompilerParams(vmem_limit_bytes=8 * 1024 * 1024),
    )(queries, payload, heads, both)
    return queries, keys, values, payload, scale.reshape(tokens)


def solution(mesh):
    return jax.shard_map(
        functools.partial(local, mesh.shape["tp"]),
        mesh=mesh,
        in_specs=(P("grp", "tp"), P("tp"), P("grp"), P(None, "tp"), P("tp", None), P("tp")),
        out_specs=(P("grp", "tp"), P("grp", "tp"), P("grp", "tp"), P("grp", "tp"), P("grp")),
        check_vma=False,
    )
```

```python
import functools
import heapq
import math

import jax
import jax.numpy as jnp
from jax import lax
from jax.experimental import pallas as pl
from jax.experimental.pallas import tpu as pltpu
from jax.sharding import PartitionSpec as P

HD = 128
KVC = 8
norm_eps = 1e-05
tiny_eps = 1e-06
rope_base = 500000.0

ROUNDS = 1
GROUP = 4
LEAD = 6.0
W_READY = 28.0
SLAB = 64
ANGLES_AT = 10.0
STEP = {"R": (0, 1), "L": (0, -1), "U": (1, 0), "D": (-1, 0)}
LINKS = "RLUD"


def plan(side, rounds, unit, slabs, lat=3.5):
    half = side // 2

    def signed(v):
        v %= side
        return v - side if v >= half else v

    def onward(kind, dy, dx, via):
        if kind in "SC":
            a, b = (dx, 0) if kind == "S" else (dy, 0)
        else:
            a, b = (dx, dy) if kind == "A" else (dy, dx)
        f1, b1, f2, b2 = ("R", "L", "U", "D") if kind in "AS" else ("U", "D", "R", "L")
        second = [f2, b2] if kind in "AB" else []
        if via is None:
            return [f1, b1] + second
        if b == 0:
            if via == f1 and a > -half:
                return [f1] + second
            if via == b1 and 0 < a < half - 1:
                return [b1] + second
            return second
        if b == -half:
            return []
        if via == f2 and (-b < half - 1 or a < 0):
            return [f2]
        if via == b2 and (b < half - 1 or (b == half - 1 and a >= 0)):
            return [b2]
        return []

    pending = {link: [] for link in LINKS}
    free = {link: 0.0 for link in LINKS}
    count = {link: 0 for link in LINKS}
    actions, heap, tick = [], [], [0]

    def push(time, what):
        tick[0] += 1
        heapq.heappush(heap, (time, tick[0], what))

    def offer(chunk, via, now):
        for link in onward(chunk[0], chunk[2], chunk[3], via):
            tick[0] += 1
            rank = -1 if chunk[0] in "SC" else abs(chunk[2] if chunk[0] == "A" else chunk[3])
            heapq.heappush(pending[link], (rank, tick[0], now, chunk))
            push(now, ("link", link))

    for rnd in range(rounds):
        for kind in "AB":
            offer((kind, rnd, 0, 0), None, 0.0)
    push(0.6, ("stat", "S"))
    left = {"S": side - 1, "C": side - 1}
    arrived = {}
    seen = set()
    while heap:
        now, _, what = heapq.heappop(heap)
        if what[0] == "link":
            link = what[1]
            if not pending[link]:
                continue
            if free[link] > now + 1e-9:
                push(free[link], what)
                continue
            _, _, ready, chunk = heapq.heappop(pending[link])
            took = 0.1 if chunk[0] in "SC" else unit
            free[link] = now + took
            k = count[link]
            count[link] += 1
            actions.append((max(ready, now - LEAD), ("send", link, k, chunk)))
            oy, ox = STEP[link]
            there = (chunk[0], chunk[1], signed(chunk[2] - oy), signed(chunk[3] - ox))
            push(free[link] + lat, ("arrive", link, k, there))
            if pending[link]:
                push(free[link], what)
        elif what[0] == "arrive":
            _, link, k, chunk = what
            assert chunk not in seen
            seen.add(chunk)
            actions.append((now, what))
            offer(chunk, link, now)
            if chunk[0] in "SC":
                left[chunk[0]] -= 1
                if left[chunk[0]] == 0:
                    actions.append((now, ("total", chunk[0])))
                    if chunk[0] == "S":
                        push(now + 0.3, ("stat", "C"))
            else:
                arrived.setdefault((chunk[1], chunk[0]), []).append((now, chunk))
        elif what[0] == "stat":
            offer((what[1], 0, 0, 0), None, now)
    assert len(seen) == 2 * rounds * (side * side - 1) + 2 * (side - 1)
    tasks = []
    for (rnd, kind), got in arrived.items():
        got = [(0.0, (kind, rnd, 0, 0))] + got
        for at in range(0, len(got), GROUP):
            part = got[at : at + GROUP]
            tasks.append((part[-1][0], rnd, ("product", kind, rnd, at == 0, [c[2:] for _, c in part])))
    tasks.sort(key=lambda t: (t[0], t[1]))
    clock = W_READY
    for ready, _, task in tasks:
        clock = max(clock + 0.45, ready)
        actions.append((clock, task))
    for i in range(slabs):
        actions.append((ANGLES_AT + i * (W_READY - ANGLES_AT) / slabs, ("angles", i)))
    end = max(t for t, _ in actions)
    for rnd in range(rounds):
        ours = [a for a in actions if a[1][0] == "product" and a[1][2] == rnd]
        final = [max((a for a in ours if a[1][1] == kind), key=lambda a: a[0]) for kind in "AB"]
        time = max(t for t, _ in final)
        actions = [a for a in actions if not any(a is f for f in final)]
        for part in ("kv", "q"):
            actions += [(time, what + (part,)) for _, what in final]
            actions.append((time, ("partial", rnd, part)))
        actions.append((time + 1.8 if time < end - 3 else end + 1, ("share", rnd)))
    order = sorted(range(len(actions)), key=lambda i: (actions[i][0], i))
    return [actions[i][1] for i in order], count


def swap_pairs(x, axis):
    size = x.shape[axis]
    even = lax.broadcasted_iota(jnp.int32, x.shape, axis) % 2 == 0
    return jnp.where(even, pltpu.roll(x, size - 1, axis), pltpu.roll(x, 1, axis))


def frequency(columns):
    index = ((columns % HD) // 2).astype(jnp.float32)
    return jnp.exp2(index * (-2.0 * math.log2(rope_base) / HD))


def body(
    side, rounds, acts, count, width, kv_heads,
    prefix, h_in, g_in, ws_in, wq_ref, wkv_ref,
    q_out, p_out, heads, both_out,
    h_ref, g_ref, ws_ref, xs, w_own, w_oth, kv_own, kv_oth, acc_q, acc_kv, part_q, part_kv,
    stat_row, stat_col, stat_oth, stat_t, cos_q, sin_q, cos_k, sin_k, share,
    send_sem, recv_sem, local_sem, pair_send, pair_recv, share_send, share_recv,
):
    tokens = h_in.shape[0]
    blocks = tokens // 128
    span = tokens // rounds
    half = span // 2
    me = lax.axis_index("tp")
    core = me % 2
    x = (me // 2) % side
    y = me // (2 * side)
    MESH = pl.DeviceIdType.MESH

    def device(yy, xx, cc):
        return {"tp": (yy * side + xx) * 2 + cc}

    partner = device(y, x, 1 - core)

    def slot_of(dy, dx):
        return ((y + dy + side) % side) * side + (x + dx + side) % side

    near = {
        link: device((y + oy + side) % side, (x + ox + side) % side, core)
        for link, (oy, ox) in STEP.items()
    }
    barrier = pltpu.get_barrier_semaphore()
    for target in near.values():
        pl.semaphore_signal(barrier, inc=1, device_id=target, device_id_type=MESH)
    ins = [
        pltpu.make_async_copy(a, b, local_sem.at[2 + i])
        for i, (a, b) in enumerate([(h_in, h_ref), (g_in, g_ref), (ws_in, ws_ref)])
    ]
    for copy in ins:
        copy.start()

    own_w = pltpu.make_async_copy(wq_ref.at[:, core], w_own, local_sem.at[0])
    own_kv = pltpu.make_async_copy(wkv_ref, kv_own, local_sem.at[1])
    own_w.start()
    own_kv.start()

    for copy in ins:
        copy.wait()
    gain = g_ref[...]
    mine = slot_of(0, 0)
    for b in range(blocks):
        rows = slice(b * 128, (b + 1) * 128)
        xs[mine, rows, :] = (h_ref[rows, :].astype(jnp.float32) * gain).astype(jnp.bfloat16)

    @pl.when(core == 1)
    def _():
        pl.semaphore_wait(barrier, 4)

    @pl.when(core == 0)
    def _():
        pl.semaphore_wait(barrier, 5)

    pl.semaphore_signal(barrier, inc=1, device_id=partner, device_id_type=MESH)

    def remote(src, dst, ssem, rsem, target):
        return pltpu.make_async_remote_copy(
            src_ref=src, dst_ref=dst, send_sem=ssem, recv_sem=rsem, device_id=target, device_id_type=MESH
        )

    give_kv = remote(wkv_ref, kv_oth, pair_send.at[0], pair_recv.at[0], partner)
    give_w = remote(wq_ref.at[:, 1 - core], w_oth, pair_send.at[1], pair_recv.at[1], partner)

    def tokens_of(kind, rnd):
        return rnd * span + (half if kind == "B" else 0)

    def place(chunk):
        kind, rnd, dy, dx = chunk
        if kind == "S":
            return stat_row.at[(x + dx + side) % side]
        if kind == "C":
            return stat_col.at[(y + dy + side) % side]
        return xs.at[slot_of(dy, dx), pl.ds(tokens_of(kind, rnd), half), :]

    def hop(link, k, chunk):
        ref = place(chunk)
        return remote(ref, ref, send_sem.at[LINKS.index(link), k], recv_sem.at[LINKS.index(link), k], near[link])

    def statistics():
        lane = lax.broadcasted_iota(jnp.int32, (128, 128), 1)
        total = jnp.zeros((128, 128), jnp.float32)
        for b in range(blocks):
            rows = slice(b * 128, (b + 1) * 128)
            wide = h_ref[rows, :].astype(jnp.float32)
            squares = jnp.sum(wide * wide, axis=1, keepdims=True)
            peak = jnp.max(jnp.abs(wide * gain), axis=1, keepdims=True)
            total = jnp.where(lane == 2 * b, squares, total)
            total = jnp.where(lane == 2 * b + 1, peak, total)
        stat_row[x] = jnp.transpose(total)[:8]

    def joined(a, b):
        even = lax.broadcasted_iota(jnp.int32, (8, 128), 0) % 2 == 0
        return jnp.where(even, a + b, jnp.maximum(a, b))

    def angles(b):
        rows = slice(b * SLAB, (b + 1) * SLAB)
        pos = prefix[0] + b * SLAB + lax.broadcasted_iota(jnp.int32, (SLAB, HD), 0)
        col = lax.broadcasted_iota(jnp.int32, (SLAB, HD), 1)
        angle = pos.astype(jnp.float32) * frequency(col)
        sine = jnp.sin(angle)
        cos_q[rows, :] = jnp.cos(angle)
        sin_q[rows, :] = jnp.where(col % 2 == 0, -sine, sine)

    piece_me = me // kv_heads
    members = 2 * side * side // kv_heads
    head_to = me % kv_heads
    head_me = me // members

    def key_angles():
        pos = prefix[0] + lax.broadcasted_iota(jnp.int32, (KVC, tokens), 1)
        row = lax.broadcasted_iota(jnp.int32, (KVC, tokens), 0)
        angle = pos.astype(jnp.float32) * frequency(piece_me * KVC + row)
        sine = jnp.sin(angle)
        cos_k[...] = jnp.cos(angle)
        sin_k[...] = jnp.where(row % 2 == 0, -sine, sine)

    def product(kind, rnd, first, places, part="both"):
        t0 = tokens_of(kind, rnd)
        slots = [slot_of(*p) for p in places]
        left = jnp.concatenate([xs[s, t0 : t0 + half, :] for s in slots], axis=1)
        if part != "kv":
            right = jnp.concatenate([jnp.concatenate([w_own[s], w_oth[s]], axis=1) for s in slots], axis=0)
            out = jnp.dot(left, right, preferred_element_type=jnp.float32)
            for who in range(2):
                piece = out[:, who * HD : (who + 1) * HD]
                if first:
                    acc_q[who, t0 : t0 + half, :] = piece
                else:
                    acc_q[who, t0 : t0 + half, :] += piece
        if part == "q":
            return
        starts = [pl.multiple_of((s * 2 + core) * width, width) for s in slots]
        rows_kv = jnp.concatenate(
            [jnp.concatenate([r[:, pl.ds(c, width)] for c in starts], axis=1) for r in (kv_own, kv_oth)], axis=0
        )
        kv = lax.dot_general(rows_kv, left, (((1,), (1,)), ((), ())), preferred_element_type=jnp.float32)
        for who in range(2):
            kvp = kv[who * 2 * KVC : (who + 1) * 2 * KVC]
            if first:
                acc_kv[who, :, t0 : t0 + half] = kvp
            else:
                acc_kv[who, :, t0 : t0 + half] += kvp

    def pair_copy(rnd, what):
        rng = pl.ds(rnd * span, span)
        if what == "kv":
            return remote(
                acc_kv.at[1, :, rng], part_kv.at[:, rng], pair_send.at[2 + rnd], pair_recv.at[2 + rnd], partner
            )
        at = 2 + rounds + rnd
        return remote(acc_q.at[1, rng, :], part_q.at[rng, :], pair_send.at[at], pair_recv.at[at], partner)

    give_stat = remote(
        stat_t, stat_oth, pair_send.at[2 + 2 * rounds], pair_recv.at[2 + 2 * rounds], partner
    )

    chips = members // 2
    far = sorted(range(chips), key=lambda o: -min(o, chips - o))

    def share_copy(rnd, m):
        rng = pl.ds(rnd * span, span)
        target = head_to * members + 2 * ((far[m] + me // 2) % chips) + piece_me % 2
        return target, remote(
            share.at[:, rng], heads.at[piece_me, :, rng], share_send.at[rnd, m], share_recv.at[rnd, piece_me],
            {"tp": target},
        )

    def passed_on(rnd, i):
        rng = pl.ds(rnd * span, span)
        p = 2 * ((far[chips - 1 - i] + y) % chips)
        mine_p, other_p = p + core, p + 1 - core
        return mine_p, other_p, remote(
            heads.at[mine_p, :, rng], heads.at[mine_p, :, rng], share_send.at[rnd, chips + i], share_recv.at[rnd, mine_p], partner
        ), remote(
            heads.at[other_p, :, rng], heads.at[other_p, :, rng], share_send.at[rnd, chips + i], share_recv.at[rnd, other_p], partner
        )

    ws_row = ws_ref[:, :HD]

    def share_round(rnd):
        rng = slice(rnd * span, (rnd + 1) * span)
        pair_copy(rnd, "kv").wait_recv()
        eye = lax.broadcasted_iota(jnp.int32, (2 * KVC, 2 * KVC), 0) == lax.broadcasted_iota(
            jnp.int32, (2 * KVC, 2 * KVC), 1
        )
        ws_col = jnp.sum(jnp.where(eye, ws_ref[:, HD:], 0.0), axis=1, keepdims=True)
        kv = (acc_kv[0, :, rng] + part_kv[:, rng]) * ws_col
        key, value = kv[:KVC], kv[KVC:]
        key = key * cos_k[:, rng] + swap_pairs(key, 0) * sin_k[:, rng]
        both = jnp.concatenate([key, value], axis=0).astype(jnp.bfloat16)
        share[:, rng] = both

        @pl.when((head_to == head_me) & (piece_me % 2 == core))
        def _():
            heads[piece_me, :, rng] = both

        for m in range(chips):
            target, copy = share_copy(rnd, m)

            @pl.when(target != me)
            def _():
                copy.start()

    @pl.when(core == 0)
    def _():
        give_kv.start()
        give_w.start()

    started = weighed = False
    for act in acts:
        if act[0] == "send":
            _, link, k, chunk = act
            if chunk[0] == "S" and not started:
                started = True
                statistics()
                key_angles()
            hop(link, k, chunk).start()
        elif act[0] == "arrive":
            _, link, k, chunk = act
            hop(link, k, chunk).wait_recv()
        elif act[0] == "total":
            if act[1] == "S":
                total = stat_row[0]
                for i in range(1, side):
                    total = joined(total, stat_row[i])
                stat_col[y] = total
            else:
                total = stat_col[0]
                for i in range(1, side):
                    total = joined(total, stat_col[i])
                stat_t[...] = total
                give_stat.start()
        elif act[0] == "angles":
            angles(act[1])
        elif act[0] == "product":
            if not weighed:
                weighed = True
                own_w.wait()
                own_kv.wait()

                @pl.when(core == 1)
                def _():
                    pl.semaphore_wait(barrier, 1)
                    give_kv.start()
                    give_w.start()

                give_kv.wait_recv()
                give_w.wait_recv()
            product(*act[1:])
        elif act[0] == "partial":
            pair_copy(act[1], act[2]).start()
        elif act[0] == "share":
            share_round(act[1])

    give_stat.wait_recv()
    total = joined(stat_t[...], stat_oth[...])
    inverse = 1.0 / jnp.sqrt(total / (width * 2 * side * side) + norm_eps)
    even = lax.broadcasted_iota(jnp.int32, (8, 128), 0) % 2 == 0
    both = jnp.where(even, inverse, total * pltpu.roll(inverse, 1, 0) + tiny_eps)
    both_out[...] = both
    columns = jnp.transpose(jnp.concatenate([both, jnp.zeros((120, 128), jnp.float32)], axis=0))
    inv = [columns[:, 2 * b : 2 * b + 1] for b in range(blocks)]
    for b in range(blocks):
        rows = slice(b * 128, (b + 1) * 128)
        weighted = h_ref[rows, :].astype(jnp.float32) * gain
        p_out[rows, :] = ((weighted * inv[b]) / columns[:, 2 * b + 1 : 2 * b + 2]).astype(jnp.bfloat16)

    for rnd in range(rounds):
        pair_copy(rnd, "q").wait_recv()
    for b in range(blocks):
        rows = slice(b * 128, (b + 1) * 128)
        q = (acc_q[0, rows, :] + part_q[rows, :]) * ws_row * inv[b]
        q_out[rows, :] = (q * cos_q[rows, :] + swap_pairs(q, 1) * sin_q[rows, :]).astype(jnp.bfloat16)

    for act in acts:
        if act[0] == "send":
            hop(*act[1:]).wait_send()
    give_kv.wait_send()
    give_w.wait_send()
    give_stat.wait_send()
    for rnd in range(rounds):
        pair_copy(rnd, "kv").wait_send()
        pair_copy(rnd, "q").wait_send()

    for rnd in range(rounds):
        for i in range(chips):
            p, _, copy, _ = passed_on(rnd, i)

            @pl.when(p * kv_heads + head_me != me)
            def _():
                copy.wait_recv()

            copy.start()
        for i in range(chips):
            passed_on(rnd, i)[3].wait_recv()
        for i in range(chips):
            passed_on(rnd, i)[2].wait_send()
    for rnd in range(rounds):
        for m in range(chips):
            target, copy = share_copy(rnd, m)

            @pl.when(target != me)
            def _():
                copy.wait_send()


def finish(blocks, members, q_in, p_in, heads, both, q_out, k_out, v_out, p_out, rs_out):
    q_out[...] = q_in[...]
    p_out[...] = p_in[...]
    both = both[...]
    rs_out[...] = jnp.concatenate([both[2 * b + 1 : 2 * b + 2] for b in range(blocks)], axis=0)
    for b in range(blocks):
        rows = slice(b * 128, (b + 1) * 128)
        got = [heads[p, :, rows].astype(jnp.float32) for p in range(members)]
        inverse = both[2 * b : 2 * b + 1]
        for out, at in ((k_out, 0), (v_out, KVC)):
            turned = jnp.concatenate([g[at : at + KVC] for g in got], axis=0) * inverse
            out[rows, :] = jnp.transpose(turned).astype(jnp.bfloat16)


def local(tp, hidden, norm_gain, prefix, w_query, w_kv, w_scale):
    tokens, width = hidden.shape
    side = math.isqrt(tp // 2)
    kv_heads = KVC * tp // HD
    members = tp // kv_heads
    rounds = ROUNDS
    acts, count = plan(side, rounds, 1.41 / rounds, tokens // SLAB)
    most = max(count.values())
    chips = tp // 2
    bf, f32 = jnp.bfloat16, jnp.float32
    vm = pl.BlockSpec(memory_space=pltpu.VMEM)
    out = jax.ShapeDtypeStruct((tokens, HD), bf)
    DMA = pltpu.SemaphoreType.DMA
    hbm = pl.BlockSpec(memory_space=pltpu.HBM)
    out_p = jax.ShapeDtypeStruct((tokens, width), bf)
    queries, payload, heads, both = pl.pallas_call(
        functools.partial(body, side, rounds, acts, count, width, kv_heads),
        out_shape=(out, out_p, jax.ShapeDtypeStruct((members, 2 * KVC, tokens), bf), jax.ShapeDtypeStruct((8, 128), f32)),
        in_specs=[pl.BlockSpec(memory_space=pltpu.SMEM)] + [hbm] * 5,
        out_specs=(vm,) * 4,
        scratch_shapes=[
            pltpu.VMEM((tokens, width), bf),
            pltpu.VMEM((1, width), f32),
            pltpu.VMEM((1, w_scale.shape[0]), f32),
            pltpu.VMEM((chips, tokens, width), bf),
            pltpu.VMEM((chips, width, HD), bf),
            pltpu.VMEM((chips, width, HD), bf),
            pltpu.VMEM(w_kv.shape, bf),
            pltpu.VMEM(w_kv.shape, bf),
            pltpu.VMEM((2, tokens, HD), f32),
            pltpu.VMEM((2, 2 * KVC, tokens), f32),
            pltpu.VMEM((tokens, HD), f32),
            pltpu.VMEM((2 * KVC, tokens), f32),
            pltpu.VMEM((side, 8, 128), f32),
            pltpu.VMEM((side, 8, 128), f32),
            pltpu.VMEM((8, 128), f32),
            pltpu.VMEM((8, 128), f32),
            pltpu.VMEM((tokens, HD), f32),
            pltpu.VMEM((tokens, HD), f32),
            pltpu.VMEM((KVC, tokens), f32),
            pltpu.VMEM((KVC, tokens), f32),
            pltpu.VMEM((2 * KVC, tokens), bf),
            DMA((4, most)),
            DMA((4, most)),
            DMA((6,)),
            DMA((3 + 2 * rounds,)),
            DMA((3 + 2 * rounds,)),
            DMA((rounds, members)),
            DMA((rounds, members)),
        ],
        compiler_params=pltpu.CompilerParams(
            collective_id=0, has_side_effects=True, vmem_limit_bytes=24 * 1024 * 1024
        ),
    )(
        prefix,
        *(
            pltpu.with_memory_space_constraint(a, pltpu.HBM)
            for a in (
                hidden,
                norm_gain.reshape(1, width),
                w_scale.reshape(1, -1),
                w_query.reshape(chips, 2, width, HD),
                w_kv,
            )
        )
    )
    queries, keys, values, payload, scale = pl.pallas_call(
        functools.partial(finish, tokens // 128, members),
        out_shape=(out, out, out, out_p, jax.ShapeDtypeStruct((tokens // 128, 128), f32)),
        in_specs=[vm] * 4,
        out_specs=(vm,) * 5,
        compiler_params=pltpu.CompilerParams(vmem_limit_bytes=8 * 1024 * 1024),
    )(queries, payload, heads, both)
    return queries, keys, values, payload, scale.reshape(tokens)


def solution(mesh):
    return jax.shard_map(
        functools.partial(local, mesh.shape["tp"]),
        mesh=mesh,
        in_specs=(P("grp", "tp"), P("tp"), P("grp"), P(None, "tp"), P("tp", None), P("tp")),
        out_specs=(P("grp", "tp"), P("grp", "tp"), P("grp", "tp"), P("grp", "tp"), P("grp")),
        check_vma=False,
    )
```

```python
import functools
import heapq
import math

import jax
import jax.numpy as jnp
from jax import lax
from jax.experimental import pallas as pl
from jax.experimental.pallas import tpu as pltpu
from jax.sharding import PartitionSpec as P

HD = 128
KVC = 8
norm_eps = 1e-05
tiny_eps = 1e-06
rope_base = 500000.0

ROUNDS = 1
GROUP = 4
LEAD = 6.0
W_READY = 28.0
SLAB = 64
ANGLES_AT = 10.0
STEP = {"R": (0, 1), "L": (0, -1), "U": (1, 0), "D": (-1, 0)}
LINKS = "RLUD"


def plan(side, rounds, unit, slabs, lat=3.5):
    half = side // 2

    def signed(v):
        v %= side
        return v - side if v >= half else v

    def onward(kind, dy, dx, via):
        if kind in "SC":
            a, b = (dx, 0) if kind == "S" else (dy, 0)
        else:
            a, b = (dx, dy) if kind == "A" else (dy, dx)
        f1, b1, f2, b2 = ("R", "L", "U", "D") if kind in "AS" else ("U", "D", "R", "L")
        second = [f2, b2] if kind in "AB" else []
        if via is None:
            return [f1, b1] + second
        if b == 0:
            if via == f1 and a > -half:
                return [f1] + second
            if via == b1 and 0 < a < half - 1:
                return [b1] + second
            return second
        if b == -half:
            return []
        if via == f2 and (-b < half - 1 or a < 0):
            return [f2]
        if via == b2 and (b < half - 1 or (b == half - 1 and a >= 0)):
            return [b2]
        return []

    pending = {link: [] for link in LINKS}
    free = {link: 0.0 for link in LINKS}
    count = {link: 0 for link in LINKS}
    actions, heap, tick = [], [], [0]

    def push(time, what):
        tick[0] += 1
        heapq.heappush(heap, (time, tick[0], what))

    def offer(chunk, via, now):
        for link in onward(chunk[0], chunk[2], chunk[3], via):
            tick[0] += 1
            rank = -1 if chunk[0] in "SC" else abs(chunk[2] if chunk[0] == "A" else chunk[3])
            heapq.heappush(pending[link], (rank, tick[0], now, chunk))
            push(now, ("link", link))

    for rnd in range(rounds):
        for kind in "AB":
            offer((kind, rnd, 0, 0), None, 0.0)
    push(0.6, ("stat", "S"))
    left = {"S": side - 1, "C": side - 1}
    arrived = {}
    seen = set()
    while heap:
        now, _, what = heapq.heappop(heap)
        if what[0] == "link":
            link = what[1]
            if not pending[link]:
                continue
            if free[link] > now + 1e-9:
                push(free[link], what)
                continue
            _, _, ready, chunk = heapq.heappop(pending[link])
            took = 0.1 if chunk[0] in "SC" else unit
            free[link] = now + took
            k = count[link]
            count[link] += 1
            actions.append((max(ready, now - LEAD), ("send", link, k, chunk)))
            oy, ox = STEP[link]
            there = (chunk[0], chunk[1], signed(chunk[2] - oy), signed(chunk[3] - ox))
            push(free[link] + lat, ("arrive", link, k, there))
            if pending[link]:
                push(free[link], what)
        elif what[0] == "arrive":
            _, link, k, chunk = what
            assert chunk not in seen
            seen.add(chunk)
            actions.append((now, what))
            offer(chunk, link, now)
            if chunk[0] in "SC":
                left[chunk[0]] -= 1
                if left[chunk[0]] == 0:
                    actions.append((now, ("total", chunk[0])))
                    if chunk[0] == "S":
                        push(now + 0.3, ("stat", "C"))
            else:
                arrived.setdefault((chunk[1], chunk[0]), []).append((now, chunk))
        elif what[0] == "stat":
            offer((what[1], 0, 0, 0), None, now)
    assert len(seen) == 2 * rounds * (side * side - 1) + 2 * (side - 1)
    tasks = []
    for (rnd, kind), got in arrived.items():
        got = [(0.0, (kind, rnd, 0, 0))] + got
        for at in range(0, len(got), GROUP):
            part = got[at : at + GROUP]
            tasks.append((part[-1][0], rnd, ("product", kind, rnd, at == 0, [c[2:] for _, c in part])))
    tasks.sort(key=lambda t: (t[0], t[1]))
    clock = W_READY
    for ready, _, task in tasks:
        clock = max(clock + 0.45, ready)
        actions.append((clock, task))
    for i in range(slabs):
        actions.append((ANGLES_AT + i * (W_READY - ANGLES_AT) / slabs, ("angles", i)))
    end = max(t for t, _ in actions)
    for rnd in range(rounds):
        ours = [a for a in actions if a[1][0] == "product" and a[1][2] == rnd]
        final = [max((a for a in ours if a[1][1] == kind), key=lambda a: a[0]) for kind in "AB"]
        time = max(t for t, _ in final)
        actions = [a for a in actions if not any(a is f for f in final)]
        for part in ("kv", "q"):
            actions += [(time, what + (part,)) for _, what in final]
            actions.append((time, ("partial", rnd, part)))
        actions.append((time + 1.8 if time < end - 3 else end + 1, ("share", rnd)))
    order = sorted(range(len(actions)), key=lambda i: (actions[i][0], i))
    return [actions[i][1] for i in order], count


def swap_pairs(x, axis):
    size = x.shape[axis]
    even = lax.broadcasted_iota(jnp.int32, x.shape, axis) % 2 == 0
    return jnp.where(even, pltpu.roll(x, size - 1, axis), pltpu.roll(x, 1, axis))


def frequency(columns):
    index = ((columns % HD) // 2).astype(jnp.float32)
    return jnp.exp2(index * (-2.0 * math.log2(rope_base) / HD))


def body(
    side, rounds, acts, count, width, kv_heads,
    prefix, h_in, g_in, ws_in, wq_ref, wkv_ref,
    q_out, p_out, heads, both_out,
    h_ref, g_ref, ws_ref, xs, w_own, w_oth, kv_own, kv_oth, acc_q, acc_kv, part_q, part_kv,
    stat_row, stat_col, stat_oth, stat_t, cos_q, sin_q, cos_k, sin_k, share,
    send_sem, recv_sem, local_sem, pair_send, pair_recv, share_send, share_recv,
):
    tokens = h_in.shape[0]
    blocks = tokens // 128
    span = tokens // rounds
    half = span // 2
    me = lax.axis_index("tp")
    core = me % 2
    x = (me // 2) % side
    y = me // (2 * side)
    MESH = pl.DeviceIdType.MESH

    def device(yy, xx, cc):
        return {"tp": (yy * side + xx) * 2 + cc}

    partner = device(y, x, 1 - core)

    def slot_of(dy, dx):
        return ((y + dy + side) % side) * side + (x + dx + side) % side

    near = {
        link: device((y + oy + side) % side, (x + ox + side) % side, core)
        for link, (oy, ox) in STEP.items()
    }
    barrier = pltpu.get_barrier_semaphore()
    for target in near.values():
        pl.semaphore_signal(barrier, inc=1, device_id=target, device_id_type=MESH)
    ins = [
        pltpu.make_async_copy(a, b, local_sem.at[2 + i])
        for i, (a, b) in enumerate([(h_in, h_ref), (g_in, g_ref), (ws_in, ws_ref)])
    ]
    for copy in ins:
        copy.start()

    own_w = pltpu.make_async_copy(wq_ref.at[:, core], w_own, local_sem.at[0])
    own_kv = pltpu.make_async_copy(wkv_ref, kv_own, local_sem.at[1])
    own_w.start()
    own_kv.start()

    for copy in ins:
        copy.wait()
    gain = g_ref[...]
    mine = slot_of(0, 0)
    for b in range(blocks):
        rows = slice(b * 128, (b + 1) * 128)
        xs[mine, rows, :] = (h_ref[rows, :].astype(jnp.float32) * gain).astype(jnp.bfloat16)

    @pl.when(core == 1)
    def _():
        pl.semaphore_wait(barrier, 4)

    @pl.when(core == 0)
    def _():
        pl.semaphore_wait(barrier, 5)

    pl.semaphore_signal(barrier, inc=1, device_id=partner, device_id_type=MESH)

    def remote(src, dst, ssem, rsem, target):
        return pltpu.make_async_remote_copy(
            src_ref=src, dst_ref=dst, send_sem=ssem, recv_sem=rsem, device_id=target, device_id_type=MESH
        )

    give_kv = remote(wkv_ref, kv_oth, pair_send.at[0], pair_recv.at[0], partner)
    give_w = remote(wq_ref.at[:, 1 - core], w_oth, pair_send.at[1], pair_recv.at[1], partner)

    def tokens_of(kind, rnd):
        return rnd * span + (half if kind == "B" else 0)

    def place(chunk):
        kind, rnd, dy, dx = chunk
        if kind == "S":
            return stat_row.at[(x + dx + side) % side]
        if kind == "C":
            return stat_col.at[(y + dy + side) % side]
        return xs.at[slot_of(dy, dx), pl.ds(tokens_of(kind, rnd), half), :]

    def hop(link, k, chunk):
        ref = place(chunk)
        return remote(ref, ref, send_sem.at[LINKS.index(link), k], recv_sem.at[LINKS.index(link), k], near[link])

    def statistics():
        lane = lax.broadcasted_iota(jnp.int32, (128, 128), 1)
        total = jnp.zeros((128, 128), jnp.float32)
        for b in range(blocks):
            rows = slice(b * 128, (b + 1) * 128)
            wide = h_ref[rows, :].astype(jnp.float32)
            squares = jnp.sum(wide * wide, axis=1, keepdims=True)
            peak = jnp.max(jnp.abs(wide * gain), axis=1, keepdims=True)
            total = jnp.where(lane == 2 * b, squares, total)
            total = jnp.where(lane == 2 * b + 1, peak, total)
        stat_row[x] = jnp.transpose(total)[:8]

    def joined(a, b):
        even = lax.broadcasted_iota(jnp.int32, (8, 128), 0) % 2 == 0
        return jnp.where(even, a + b, jnp.maximum(a, b))

    def angles(b):
        rows = slice(b * SLAB, (b + 1) * SLAB)
        pos = prefix[0] + b * SLAB + lax.broadcasted_iota(jnp.int32, (SLAB, HD), 0)
        col = lax.broadcasted_iota(jnp.int32, (SLAB, HD), 1)
        angle = pos.astype(jnp.float32) * frequency(col)
        sine = jnp.sin(angle)
        cos_q[rows, :] = jnp.cos(angle)
        sin_q[rows, :] = jnp.where(col % 2 == 0, -sine, sine)

    piece_me = me // kv_heads
    members = 2 * side * side // kv_heads
    head_to = me % kv_heads
    head_me = me // members

    def key_angles():
        pos = prefix[0] + lax.broadcasted_iota(jnp.int32, (KVC, tokens), 1)
        row = lax.broadcasted_iota(jnp.int32, (KVC, tokens), 0)
        angle = pos.astype(jnp.float32) * frequency(piece_me * KVC + row)
        sine = jnp.sin(angle)
        cos_k[...] = jnp.cos(angle)
        sin_k[...] = jnp.where(row % 2 == 0, -sine, sine)

    def product(kind, rnd, first, places, part="both"):
        t0 = tokens_of(kind, rnd)
        slots = [slot_of(*p) for p in places]
        left = jnp.concatenate([xs[s, t0 : t0 + half, :] for s in slots], axis=1)
        if part != "kv":
            right = jnp.concatenate([jnp.concatenate([w_own[s], w_oth[s]], axis=1) for s in slots], axis=0)
            out = jnp.dot(left, right, preferred_element_type=jnp.float32)
            for who in range(2):
                piece = out[:, who * HD : (who + 1) * HD]
                if first:
                    acc_q[who, t0 : t0 + half, :] = piece
                else:
                    acc_q[who, t0 : t0 + half, :] += piece
        if part == "q":
            return
        starts = [pl.multiple_of((s * 2 + core) * width, width) for s in slots]
        rows_kv = jnp.concatenate(
            [jnp.concatenate([r[:, pl.ds(c, width)] for c in starts], axis=1) for r in (kv_own, kv_oth)], axis=0
        )
        kv = lax.dot_general(rows_kv, left, (((1,), (1,)), ((), ())), preferred_element_type=jnp.float32)
        for who in range(2):
            kvp = kv[who * 2 * KVC : (who + 1) * 2 * KVC]
            if first:
                acc_kv[who, :, t0 : t0 + half] = kvp
            else:
                acc_kv[who, :, t0 : t0 + half] += kvp

    def pair_copy(rnd, what):
        rng = pl.ds(rnd * span, span)
        if what == "kv":
            return remote(
                acc_kv.at[1, :, rng], part_kv.at[:, rng], pair_send.at[2 + rnd], pair_recv.at[2 + rnd], partner
            )
        at = 2 + rounds + rnd
        return remote(acc_q.at[1, rng, :], part_q.at[rng, :], pair_send.at[at], pair_recv.at[at], partner)

    give_stat = remote(
        stat_t, stat_oth, pair_send.at[2 + 2 * rounds], pair_recv.at[2 + 2 * rounds], partner
    )

    chips = members // 2
    far = sorted(range(chips), key=lambda o: -min(o, chips - o))

    def share_copy(rnd, m):
        rng = pl.ds(rnd * span, span)
        target = head_to * members + 2 * ((far[m] + me // 2) % chips) + piece_me % 2
        return target, remote(
            share.at[:, rng], heads.at[piece_me, :, rng], share_send.at[rnd, m], share_recv.at[rnd, piece_me],
            {"tp": target},
        )

    def passed_on(rnd, i):
        rng = pl.ds(rnd * span, span)
        p = 2 * ((far[chips - 1 - i] + y) % chips)
        mine_p, other_p = p + core, p + 1 - core
        return mine_p, other_p, remote(
            heads.at[mine_p, :, rng], heads.at[mine_p, :, rng], share_send.at[rnd, chips + i], share_recv.at[rnd, mine_p], partner
        ), remote(
            heads.at[other_p, :, rng], heads.at[other_p, :, rng], share_send.at[rnd, chips + i], share_recv.at[rnd, other_p], partner
        )

    ws_row = ws_ref[:, :HD]

    def share_round(rnd):
        rng = slice(rnd * span, (rnd + 1) * span)
        pair_copy(rnd, "kv").wait_recv()
        eye = lax.broadcasted_iota(jnp.int32, (2 * KVC, 2 * KVC), 0) == lax.broadcasted_iota(
            jnp.int32, (2 * KVC, 2 * KVC), 1
        )
        ws_col = jnp.sum(jnp.where(eye, ws_ref[:, HD:], 0.0), axis=1, keepdims=True)
        kv = (acc_kv[0, :, rng] + part_kv[:, rng]) * ws_col
        key, value = kv[:KVC], kv[KVC:]
        key = key * cos_k[:, rng] + swap_pairs(key, 0) * sin_k[:, rng]
        both = jnp.concatenate([key, value], axis=0).astype(jnp.bfloat16)
        share[:, rng] = both

        @pl.when((head_to == head_me) & (piece_me % 2 == core))
        def _():
            heads[piece_me, :, rng] = both

        for m in range(chips):
            target, copy = share_copy(rnd, m)

            @pl.when(target != me)
            def _():
                copy.start()

    def scales():
        give_stat.wait_recv()
        total = joined(stat_t[...], stat_oth[...])
        inverse = 1.0 / jnp.sqrt(total / (width * 2 * side * side) + norm_eps)
        even = lax.broadcasted_iota(jnp.int32, (8, 128), 0) % 2 == 0
        both = jnp.where(even, inverse, total * pltpu.roll(inverse, 1, 0) + tiny_eps)
        both_out[...] = both
        columns = jnp.transpose(jnp.concatenate([both, jnp.zeros((120, 128), jnp.float32)], axis=0))
        inv = [columns[:, 2 * b : 2 * b + 1] for b in range(blocks)]
        for b in range(blocks):
            rows = slice(b * 128, (b + 1) * 128)
            weighted = h_ref[rows, :].astype(jnp.float32) * gain
            p_out[rows, :] = ((weighted * inv[b]) / columns[:, 2 * b + 1 : 2 * b + 2]).astype(jnp.bfloat16)
        return inv

    @pl.when(core == 0)
    def _():
        give_kv.start()
        give_w.start()

    started = weighed = False
    for act in acts:
        if act[0] == "send":
            _, link, k, chunk = act
            if chunk[0] == "S" and not started:
                started = True
                statistics()
                key_angles()
            hop(link, k, chunk).start()
        elif act[0] == "arrive":
            _, link, k, chunk = act
            hop(link, k, chunk).wait_recv()
        elif act[0] == "total":
            if act[1] == "S":
                total = stat_row[0]
                for i in range(1, side):
                    total = joined(total, stat_row[i])
                stat_col[y] = total
            else:
                total = stat_col[0]
                for i in range(1, side):
                    total = joined(total, stat_col[i])
                stat_t[...] = total
                give_stat.start()
        elif act[0] == "angles":
            angles(act[1])
        elif act[0] == "product":
            if not weighed:
                weighed = True
                own_w.wait()
                own_kv.wait()

                @pl.when(core == 1)
                def _():
                    pl.semaphore_wait(barrier, 1)
                    give_kv.start()
                    give_w.start()

                give_kv.wait_recv()
                give_w.wait_recv()
            product(*act[1:])
        elif act[0] == "partial":
            pair_copy(act[1], act[2]).start()
        elif act[0] == "share":
            if act[1] == rounds - 1:
                inv = scales()
            share_round(act[1])

    for rnd in range(rounds):
        pair_copy(rnd, "q").wait_recv()
    for b in range(blocks):
        rows = slice(b * 128, (b + 1) * 128)
        q = (acc_q[0, rows, :] + part_q[rows, :]) * ws_row * inv[b]
        q_out[rows, :] = (q * cos_q[rows, :] + swap_pairs(q, 1) * sin_q[rows, :]).astype(jnp.bfloat16)

    for act in acts:
        if act[0] == "send":
            hop(*act[1:]).wait_send()
    give_kv.wait_send()
    give_w.wait_send()
    give_stat.wait_send()
    for rnd in range(rounds):
        pair_copy(rnd, "kv").wait_send()
        pair_copy(rnd, "q").wait_send()

    for rnd in range(rounds):
        for i in range(chips):
            p, _, copy, _ = passed_on(rnd, i)

            @pl.when(p * kv_heads + head_me != me)
            def _():
                copy.wait_recv()

            copy.start()
        for i in range(chips):
            passed_on(rnd, i)[3].wait_recv()
        for i in range(chips):
            passed_on(rnd, i)[2].wait_send()
    for rnd in range(rounds):
        for m in range(chips):
            target, copy = share_copy(rnd, m)

            @pl.when(target != me)
            def _():
                copy.wait_send()


def finish(blocks, members, q_in, p_in, heads, both, q_out, k_out, v_out, p_out, rs_out):
    q_out[...] = q_in[...]
    p_out[...] = p_in[...]
    both = both[...]
    rs_out[...] = jnp.concatenate([both[2 * b + 1 : 2 * b + 2] for b in range(blocks)], axis=0)
    for b in range(blocks):
        rows = slice(b * 128, (b + 1) * 128)
        got = [heads[p, :, rows].astype(jnp.float32) for p in range(members)]
        inverse = both[2 * b : 2 * b + 1]
        for out, at in ((k_out, 0), (v_out, KVC)):
            turned = jnp.concatenate([g[at : at + KVC] for g in got], axis=0) * inverse
            out[rows, :] = jnp.transpose(turned).astype(jnp.bfloat16)


def local(tp, hidden, norm_gain, prefix, w_query, w_kv, w_scale):
    tokens, width = hidden.shape
    side = math.isqrt(tp // 2)
    kv_heads = KVC * tp // HD
    members = tp // kv_heads
    rounds = ROUNDS
    acts, count = plan(side, rounds, 1.41 / rounds, tokens // SLAB)
    most = max(count.values())
    chips = tp // 2
    bf, f32 = jnp.bfloat16, jnp.float32
    vm = pl.BlockSpec(memory_space=pltpu.VMEM)
    out = jax.ShapeDtypeStruct((tokens, HD), bf)
    DMA = pltpu.SemaphoreType.DMA
    hbm = pl.BlockSpec(memory_space=pltpu.HBM)
    out_p = jax.ShapeDtypeStruct((tokens, width), bf)
    queries, payload, heads, both = pl.pallas_call(
        functools.partial(body, side, rounds, acts, count, width, kv_heads),
        out_shape=(out, out_p, jax.ShapeDtypeStruct((members, 2 * KVC, tokens), bf), jax.ShapeDtypeStruct((8, 128), f32)),
        in_specs=[pl.BlockSpec(memory_space=pltpu.SMEM)] + [hbm] * 5,
        out_specs=(vm,) * 4,
        scratch_shapes=[
            pltpu.VMEM((tokens, width), bf),
            pltpu.VMEM((1, width), f32),
            pltpu.VMEM((1, w_scale.shape[0]), f32),
            pltpu.VMEM((chips, tokens, width), bf),
            pltpu.VMEM((chips, width, HD), bf),
            pltpu.VMEM((chips, width, HD), bf),
            pltpu.VMEM(w_kv.shape, bf),
            pltpu.VMEM(w_kv.shape, bf),
            pltpu.VMEM((2, tokens, HD), f32),
            pltpu.VMEM((2, 2 * KVC, tokens), f32),
            pltpu.VMEM((tokens, HD), f32),
            pltpu.VMEM((2 * KVC, tokens), f32),
            pltpu.VMEM((side, 8, 128), f32),
            pltpu.VMEM((side, 8, 128), f32),
            pltpu.VMEM((8, 128), f32),
            pltpu.VMEM((8, 128), f32),
            pltpu.VMEM((tokens, HD), f32),
            pltpu.VMEM((tokens, HD), f32),
            pltpu.VMEM((KVC, tokens), f32),
            pltpu.VMEM((KVC, tokens), f32),
            pltpu.VMEM((2 * KVC, tokens), bf),
            DMA((4, most)),
            DMA((4, most)),
            DMA((6,)),
            DMA((3 + 2 * rounds,)),
            DMA((3 + 2 * rounds,)),
            DMA((rounds, members)),
            DMA((rounds, members)),
        ],
        compiler_params=pltpu.CompilerParams(
            collective_id=0, has_side_effects=True, vmem_limit_bytes=24 * 1024 * 1024
        ),
    )(
        prefix,
        *(
            pltpu.with_memory_space_constraint(a, pltpu.HBM)
            for a in (
                hidden,
                norm_gain.reshape(1, width),
                w_scale.reshape(1, -1),
                w_query.reshape(chips, 2, width, HD),
                w_kv,
            )
        )
    )
    queries, keys, values, payload, scale = pl.pallas_call(
        functools.partial(finish, tokens // 128, members),
        out_shape=(out, out, out, out_p, jax.ShapeDtypeStruct((tokens // 128, 128), f32)),
        in_specs=[vm] * 4,
        out_specs=(vm,) * 5,
        compiler_params=pltpu.CompilerParams(vmem_limit_bytes=8 * 1024 * 1024),
    )(queries, payload, heads, both)
    return queries, keys, values, payload, scale.reshape(tokens)


def solution(mesh):
    return jax.shard_map(
        functools.partial(local, mesh.shape["tp"]),
        mesh=mesh,
        in_specs=(P("grp", "tp"), P("tp"), P("grp"), P(None, "tp"), P("tp", None), P("tp")),
        out_specs=(P("grp", "tp"), P("grp", "tp"), P("grp", "tp"), P("grp", "tp"), P("grp")),
        check_vma=False,
    )
```
